32 devices in a mesh: group: 2 (over core), ctx: 8 (over z, x), mp: 2 (over y).
Axes of the slice: x: 2, y: 2, z: 4, core: 2. Of those that a mesh axis runs over, the one named last changes fastest.
Arguments:
- token_ids: int32 [2, 1024], P('group', 'ctx'), may hold values from 0 to 127
- span_offset: int32 [1], replicated, may hold values from 0 to 3071
- shard_lengths: int32 [8], P('ctx'), may hold values from 1 to 384
- embed_table: bfloat16 [128, 2560], P(None, 'mp'), may hold values from -6 to 6
- norm_gain: bfloat16 [2560], P('mp'), may hold values from 0.25 to 1.75
- query_weight: bfloat16 [2560, 2560], P('mp'), may hold values from -0.25 to 0.25
- key_weight: bfloat16 [2560, 2560], P('mp'), may hold values from -0.25 to 0.25
- value_weight: bfloat16 [2560, 2560], P('mp'), may hold values from -0.125 to 0.125
- cache_keys: bfloat16 [3072, 2560], P('ctx', 'mp'), may hold values from -440 to 440
- cache_values: bfloat16 [3072, 2560], P('ctx', 'mp'), may hold values from -6 to 6
Outputs:
- attended: bfloat16 [2, 1024, 2560], P('group', 'ctx', 'mp')
The draws below stay inside these ranges and needn't reach their ends.
All inputs are finite; a program needn't handle non-finite values.
Results may differ from the reference program's by a relative error of at most 0.012.
The reference program's roundings to bfloat16 on the way (of `normal_rows`) count: a program that leaves them out, or rounds other values in their place, can miss the bound.
Values may be sent and summed in bfloat16 or wider, within the bound.
A program may use at most 256 MiB of HBM per device.

```python
import math
import jax
import jax.numpy as jnp
from jax import lax

D = 2560
HEADS = 32
HD = 80
VOCAB = 128
PROT = 256
STEPS = 4
ROWS_DEV = 128
CACHE_DEV = 384
SPAN = 1024
CONTEXT = 3072
N_CTX = 8


def draw_cache_keys(key, part):
    normal_part = jax.random.normal(key, (CONTEXT, D), jnp.float32) * 2.0
    result = jnp.clip(normal_part, -12.0, 12.0)
    return result.astype(jnp.bfloat16)


def plant(values, own_key, least, high):
    dims = values.shape
    index_at = [jax.random.randint(jax.random.fold_in(own_key, axis), (), 0, dims[axis]) for axis in range(len(dims))]
    values = values.at[tuple(index_at)].set(least)
    longest = dims.index(max(dims))
    index_at[longest] = (index_at[longest] + 1) % dims[longest]
    return values.at[tuple(index_at)].set(high)


def levels(rng, extent, shards, least, top_value):
    gain, own = 1.0, jax.random.fold_in(rng, 6)
    for axis_at, shards_of in shards:
        draws = jnp.exp(jax.random.uniform(jax.random.fold_in(own, axis_at), (shards_of,), jnp.float32, least / len(shards), top_value / len(shards)))
        gain = gain * jnp.repeat(draws, extent[axis_at] // shards_of).reshape([-1 if axis == axis_at else 1 for axis in range(len(extent))])
    return gain


def normal_values(stream_key, extent, width, reach, shards=(), held_as=jnp.bfloat16):
    level = levels(stream_key, extent, shards, -0.22, 0.18) if shards else 1.0
    drawn = jax.random.normal(stream_key, extent, jnp.float32) * width * level
    return jnp.minimum(jnp.maximum(drawn, -reach), reach).astype(held_as)


def setup_inputs(seed: int = 0) -> dict:
    key_list = jax.random.split(jax.random.key(seed), 11)
    return {
        "token_ids": plant(jax.random.randint(key_list[0], (2, SPAN), 0, VOCAB), jax.random.fold_in(key_list[0], 1), 0, VOCAB - 1).astype(jnp.int32),
        "span_offset": jax.random.randint(key_list[1], (1,), 0, CONTEXT).astype(jnp.int32),
        "shard_lengths": plant(jax.random.randint(key_list[2], (N_CTX,), 1, CACHE_DEV + 1), jax.random.fold_in(key_list[2], 1), 1, CACHE_DEV).astype(jnp.int32),
        "embed_table": normal_values(key_list[3], (VOCAB, D), 1.0, 6.0, ((1, 2),)),
        "norm_gain": jnp.clip(1.0 + 0.15 * jax.random.normal(key_list[4], (D,), jnp.float32), 0.25, 1.75).astype(jnp.bfloat16),
        "query_weight": normal_values(key_list[5], (D, D), (D // 4) ** -0.5, 0.25, ((0, 2),)),
        "key_weight": normal_values(key_list[6], (D, D), (D // 4) ** -0.5, 0.25, ((0, 2),)),
        "value_weight": normal_values(key_list[7], (D, D), D ** -0.5, 0.125, ((0, 2),)),
        "cache_keys": draw_cache_keys(jax.random.fold_in(key_list[10], 71), 0),
        "cache_values": normal_values(key_list[9], (CONTEXT, D), 1.0, 6.0, ((0, 8), (1, 2))),
    }


def rotate(values_in, positions):
    row_count = values_in.shape[0]
    head_count = values_in.shape[1] // HD
    quarter = HD // 4
    column = (positions % PROT).astype(jnp.float32)
    homolog = (positions // PROT).astype(jnp.float32)
    frequency = 10000.0 ** (-jnp.arange(quarter, dtype=jnp.float32) / quarter)
    angles = jnp.stack([column[:, None] * frequency, homolog[:, None] * frequency], 1)
    cosine = jnp.cos(angles)[:, None, :, None, :]
    sine_table = jnp.sin(angles)[:, None, :, None, :]
    pieces = values_in.reshape(row_count, head_count, 2, 2, quarter)
    partner = jnp.stack([-pieces[:, :, :, 1], pieces[:, :, :, 0]], 3)
    return (pieces * cosine + partner * sine_table).reshape(row_count, head_count * HD)

def normed(embedded, gain_vector):
    mean_square = lax.optimization_barrier(jnp.mean(embedded * embedded, -1, keepdims=True))
    return (embedded * lax.rsqrt(mean_square + 1e-05) * gain_vector.astype(jnp.float32)).astype(jnp.bfloat16)

def reference(token_ids, span_offset, shard_lengths, embed_table, norm_gain, query_weight, key_weight, value_weight, cache_keys, cache_values):
    score_scale = 1.0 / math.sqrt(HD)
    embedded = embed_table[token_ids].astype(jnp.float32).reshape(2 * SPAN, D)
    normal_rows = normed(embedded, norm_gain)
    query_full = jnp.dot(normal_rows, query_weight, preferred_element_type=jnp.float32)
    key_full = jnp.dot(normal_rows, key_weight, preferred_element_type=jnp.float32)
    value_full = jnp.dot(normal_rows, value_weight, preferred_element_type=jnp.float32)
    row_iota = jnp.arange(SPAN, dtype=jnp.int32)
    offset_value = span_offset[0]
    positions = jnp.concatenate([offset_value + row_iota, offset_value + SPAN + row_iota % STEPS])
    queries = rotate(query_full, positions).astype(jnp.bfloat16).reshape(2, SPAN, HEADS, HD)
    new_keys = rotate(key_full, positions).astype(jnp.bfloat16).reshape(2, SPAN, HEADS, HD)
    new_values = value_full.astype(jnp.bfloat16).reshape(2, SPAN, HEADS, HD)
    cache_k = cache_keys.reshape(CONTEXT, HEADS, HD)
    cache_v = cache_values.reshape(CONTEXT, HEADS, HD)
    key_slots = CACHE_DEV + ROWS_DEV
    slot = jnp.arange(key_slots, dtype=jnp.int32)
    results = []
    for group_index in range(2):
        query_group = queries[group_index].astype(jnp.float32)

        def shard_step(carry, shard):
            big_max, big_sum, big_acc = carry
            start_cache = (shard * CACHE_DEV).astype(jnp.int32)
            start_span = (shard * ROWS_DEV).astype(jnp.int32)
            keys_here = jnp.concatenate([lax.dynamic_slice_in_dim(cache_k, start_cache, CACHE_DEV, 0), lax.dynamic_slice_in_dim(new_keys[0], start_span, ROWS_DEV, 0)], 0)
            values_here = jnp.concatenate([lax.dynamic_slice_in_dim(cache_v, start_cache, CACHE_DEV, 0), lax.dynamic_slice_in_dim(new_values[0], start_span, ROWS_DEV, 0)], 0)
            scores = jnp.einsum('qhd,khd->hqk', query_group, keys_here.astype(jnp.float32)) * score_scale
            cache_live = (slot < CACHE_DEV) & (slot < shard_lengths[shard])
            span_index = start_span + slot - CACHE_DEV
            span_seen = (slot >= CACHE_DEV)[None, :] & ((group_index == 1) | (span_index[None, :] <= row_iota[:, None]))
            visible = (cache_live[None, :] | span_seen)[None]
            shard_max = lax.optimization_barrier(jnp.max(jnp.where(visible, scores, -1e+30), -1))
            weights = jnp.where(visible, jnp.exp(scores - shard_max[..., None]), 0.0)
            shard_sum = lax.optimization_barrier(jnp.sum(weights, -1))
            shard_acc = jnp.einsum('hqk,khd->hqd', weights.astype(jnp.bfloat16).astype(jnp.float32), values_here.astype(jnp.float32))
            new_max = jnp.maximum(big_max, shard_max)
            keep_old = jnp.exp(big_max - new_max)
            keep_new = jnp.exp(shard_max - new_max)
            return ((new_max, big_sum * keep_old + shard_sum * keep_new, big_acc * keep_old[..., None] + shard_acc * keep_new[..., None]), None)
        start_state = (jnp.full((HEADS, SPAN), -1e+30, jnp.float32), jnp.zeros((HEADS, SPAN), jnp.float32), jnp.zeros((HEADS, SPAN, HD), jnp.float32))
        (whole_max, whole_sum, whole_acc), unused = lax.scan(shard_step, start_state, jnp.arange(N_CTX, dtype=jnp.int32))
        cands = SPAN // STEPS
        own_q = query_group.reshape(cands, STEPS, HEADS, HD)
        own_k = new_keys[group_index].astype(jnp.float32).reshape(cands, STEPS, HEADS, HD)
        own_v = new_values[group_index].astype(jnp.float32).reshape(cands, STEPS, HEADS, HD)
        own_scores = jnp.einsum('ashd,athd->ahst', own_q, own_k) * score_scale
        step_iota = jnp.arange(STEPS, dtype=jnp.int32)
        own_visible = (step_iota[None, :] <= step_iota[:, None]) & (group_index == 1)
        own_max = lax.optimization_barrier(jnp.max(jnp.where(own_visible, own_scores, -1e+30), -1))
        own_max_rows = own_max.transpose(1, 0, 2).reshape(HEADS, SPAN)
        final_max = jnp.maximum(whole_max, own_max_rows)
        keep_old = jnp.exp(whole_max - final_max)
        final_cand = final_max.reshape(HEADS, cands, STEPS).transpose(1, 0, 2)
        own_weights = jnp.where(own_visible, jnp.exp(own_scores - final_cand[..., None]), 0.0)
        own_sum = lax.optimization_barrier(jnp.sum(own_weights, -1)).transpose(1, 0, 2).reshape(HEADS, SPAN)
        own_acc = jnp.einsum('ahst,athd->hasd', own_weights.astype(jnp.bfloat16).astype(jnp.float32), own_v).reshape(HEADS, SPAN, HD)
        numer = whole_acc * keep_old[..., None] + own_acc
        denom = whole_sum * keep_old + own_sum
        output = (numer / denom[..., None]).transpose(1, 0, 2).reshape(SPAN, D)
        results.append(output.astype(jnp.bfloat16))
    return jnp.stack(results, 0)
```

```python
import math

import jax
import jax.numpy as jnp
from jax import lax
from jax.experimental import pallas as pl
from jax.experimental.pallas import tpu as pltpu
from jax.sharding import PartitionSpec as P

D = 2560
HD = 80
PROT = 256
STEPS = 4


def passed_along(value, axis, steps):
    count = lax.axis_size(axis)
    first, last = (max(0, -steps), min(count, count - steps))
    return lax.ppermute(value, axis, [(source, source + steps) for source in range(first, last)])


def rotate(values_in, positions):
    row_count = values_in.shape[0]
    head_count = values_in.shape[1] // HD
    quarter = HD // 4
    column = (positions % PROT).astype(jnp.float32)
    homolog = (positions // PROT).astype(jnp.float32)
    frequency = 10000.0 ** (-jnp.arange(quarter, dtype=jnp.float32) / quarter)
    angles = jnp.stack([column[:, None] * frequency, homolog[:, None] * frequency], 1)
    cosine = jnp.cos(angles)[:, None, :, None, :]
    sine_table = jnp.sin(angles)[:, None, :, None, :]
    pieces = values_in.reshape(row_count, head_count, 2, 2, quarter)
    partner = jnp.stack([-pieces[:, :, :, 1], pieces[:, :, :, 0]], 3)
    return (pieces * cosine + partner * sine_table).reshape(row_count, head_count * HD)


def block_partial(
    query_block, start, all_keys, all_values, live_length, span_base, cache_count, decoding
):
    block_rows = query_block.shape[0]
    head_count = query_block.shape[1] // HD
    key_slots = all_keys.shape[0]
    query_heads = query_block.reshape(block_rows, head_count, HD)
    key_heads = all_keys.reshape(key_slots, head_count, HD)
    value_heads = all_values.reshape(key_slots, head_count, HD)
    scores = jnp.einsum(
        "qhd,khd->hqk", query_heads, key_heads, preferred_element_type=jnp.float32
    ) * (1.0 / math.sqrt(HD))
    slot = jnp.arange(key_slots, dtype=jnp.int32)
    query_index = start + jnp.arange(block_rows, dtype=jnp.int32)
    cache_live = (slot < cache_count) & (slot < live_length)
    span_index = span_base + slot - cache_count
    span_seen = (slot >= cache_count)[None, :] & (
        decoding | (span_index[None, :] <= query_index[:, None])
    )
    visible = (cache_live[None, :] | span_seen)[None]
    block_max = jnp.max(jnp.where(visible, scores, -1e30), -1)
    weights = jnp.where(visible, jnp.exp(scores - block_max[..., None]), 0.0)
    block_sum = jnp.sum(weights, -1)
    block_acc = jnp.einsum(
        "hqk,khd->qhd",
        weights.astype(jnp.bfloat16),
        value_heads,
        preferred_element_type=jnp.float32,
    )
    return (block_max.T, block_sum.T, block_acc.reshape(block_rows, head_count * HD))


def local(
    token_ids,
    span_offset,
    shard_lengths,
    embed_table,
    norm_gain,
    query_weight,
    key_weight,
    value_weight,
    cache_keys,
    cache_values,
):
    token_row = token_ids[0]
    row_count = token_row.shape[0]
    ctx_count = lax.axis_size("ctx")
    ctx_index = lax.axis_index("ctx")
    decoding = lax.axis_index("group") == 1
    one_hot = (
        token_row[:, None] == jnp.arange(embed_table.shape[0], dtype=jnp.int32)[None, :]
    ).astype(jnp.bfloat16)
    embedded = jnp.dot(one_hot, embed_table, preferred_element_type=jnp.float32)
    square_sum = lax.psum(jnp.sum(embedded * embedded, 1), "mp")
    normal_rows = (
        embedded * lax.rsqrt(square_sum / D + 1e-05)[:, None] * norm_gain.astype(jnp.float32)
    ).astype(jnp.bfloat16)
    query_part = jnp.dot(normal_rows, query_weight, preferred_element_type=jnp.float32)
    key_part = jnp.dot(normal_rows, key_weight, preferred_element_type=jnp.float32)
    value_part = jnp.dot(normal_rows, value_weight, preferred_element_type=jnp.float32)
    query_full, key_full, value_full = (
        lax.psum_scatter(query_part, "mp", scatter_dimension=1, tiled=True),
        lax.psum_scatter(key_part, "mp", scatter_dimension=1, tiled=True),
        lax.psum_scatter(value_part, "mp", scatter_dimension=1, tiled=True),
    )
    offset_value = span_offset[0]
    local_iota = jnp.arange(row_count, dtype=jnp.int32)
    positions = jnp.where(
        decoding,
        offset_value + row_count * ctx_count + local_iota % STEPS,
        offset_value + ctx_index * row_count + local_iota,
    )
    queries = rotate(query_full, positions).astype(jnp.bfloat16)
    new_keys = rotate(key_full, positions).astype(jnp.bfloat16)
    new_values = value_full.astype(jnp.bfloat16)
    width = queries.shape[1]
    head_count = width // HD
    span_keys, span_values = passed_along((new_keys, new_values), "group", 1)
    block_keys = jnp.where(decoding, span_keys, new_keys)
    block_values = jnp.where(decoding, span_values, new_values)
    cache_count = cache_keys.shape[0]
    all_keys = jnp.concatenate([cache_keys, block_keys], 0)
    all_values = jnp.concatenate([cache_values, block_values], 0)
    live_length = shard_lengths[0]
    span_base = ctx_index * row_count
    gathered = lax.all_gather(queries, "ctx", axis=0, tiled=True)
    total = gathered.shape[0]
    block_rows = math.gcd(total, 512)
    block_count = total // block_rows
    block_starts = jnp.arange(block_count, dtype=jnp.int32) * block_rows

    def one_block(pair):
        return block_partial(
            pair[0], pair[1], all_keys, all_values, live_length, span_base, cache_count, decoding
        )

    maxima, totals, sums = lax.map(
        one_block, (gathered.reshape(block_count, block_rows, width), block_starts)
    )
    maxima = maxima.reshape(total, head_count)
    totals = totals.reshape(total, head_count)
    sums = sums.reshape(total, width)
    got_max, got_sum, got_acc = (
        lax.all_to_all(maxima[None], "ctx", split_axis=1, concat_axis=0, tiled=True),
        lax.all_to_all(totals[None], "ctx", split_axis=1, concat_axis=0, tiled=True),
        lax.all_to_all(sums[None], "ctx", split_axis=1, concat_axis=0, tiled=True),
    )
    whole_max = jnp.max(got_max, 0)
    rescale = jnp.exp(got_max - whole_max[None])
    whole_sum = jnp.sum(rescale * got_sum, 0)
    whole_acc = jnp.sum(got_acc * jnp.repeat(rescale, HD, axis=2), 0)
    cands = row_count // STEPS
    own_q = queries.reshape(cands, STEPS, head_count, HD)
    own_k = new_keys.reshape(cands, STEPS, head_count, HD)
    own_v = new_values.reshape(cands, STEPS, head_count, HD)
    own_scores = jnp.einsum("ashd,athd->ahst", own_q, own_k, preferred_element_type=jnp.float32) * (
        1.0 / math.sqrt(HD)
    )
    step_iota = jnp.arange(STEPS, dtype=jnp.int32)
    own_visible = (step_iota[None, :] <= step_iota[:, None]) & decoding
    own_max = jnp.max(jnp.where(own_visible, own_scores, -1e30), -1)
    final_max = jnp.maximum(whole_max, own_max.transpose(0, 2, 1).reshape(row_count, head_count))
    keep_old = jnp.exp(whole_max - final_max)
    final_cand = final_max.reshape(cands, STEPS, head_count).transpose(0, 2, 1)
    own_weights = jnp.where(own_visible, jnp.exp(own_scores - final_cand[..., None]), 0.0)
    own_sum = jnp.sum(own_weights, -1).transpose(0, 2, 1).reshape(row_count, head_count)
    own_acc = jnp.einsum(
        "ahst,athd->ashd",
        own_weights.astype(jnp.bfloat16),
        own_v,
        preferred_element_type=jnp.float32,
    ).reshape(row_count, width)
    numer = whole_acc * jnp.repeat(keep_old, HD, axis=1) + own_acc
    denom = whole_sum * keep_old + own_sum
    output = numer / jnp.repeat(denom, HD, axis=1)
    return output.astype(jnp.bfloat16)[None]


MESH_ID = pl.DeviceIdType.MESH
META = 16
WINDOW = 256


def exchange_kernel(
    packed, embed, gain, wq, wk, wv, kv, table, wbuf, ss_out, ss_in, part_out, part_in, wsem, own_sem,
    send_sem, recv_sem, relay_send, relay_recv, mp_send, mp_recv,
):
    count = packed.shape[0]
    span = packed.shape[1] - META
    group, ctx, mp = lax.axis_index("group"), lax.axis_index("ctx"), lax.axis_index("mp")
    half = wq.shape[1] // 2
    first = pl.multiple_of(ctx * span // 128 * 128, 128)
    barrier = pltpu.get_barrier_semaphore()
    for step in range(1, count):
        pl.semaphore_signal(
            barrier, inc=1, device_id={"ctx": lax.rem(ctx + step, count)}, device_id_type=MESH_ID
        )
    pl.semaphore_signal(barrier, inc=1, device_id={"group": 1 - group}, device_id_type=MESH_ID)
    pl.semaphore_signal(barrier, inc=1, device_id={"mp": 1 - mp}, device_id_type=MESH_ID)
    loads = []
    for slot in range(6):
        side = 1 - mp if slot < 3 else mp
        weight = (wq, wk, wv)[slot % 3]
        column = pl.multiple_of(side * half + first, 128)
        loads.append(
            pltpu.make_async_copy(
                weight.at[:, pl.ds(column, WINDOW)], wbuf.at[slot], wsem.at[slot]
            )
        )
        loads[-1].start()
    mine = pltpu.make_async_copy(packed.at[ctx], kv.at[group, ctx], own_sem)
    mine.start()
    pl.semaphore_wait(barrier, count + 1)
    sends = []
    for step in range(1, count):
        target = lax.rem(ctx + step, count)
        sends.append(
            pltpu.make_async_remote_copy(
                src_ref=packed.at[target],
                dst_ref=kv.at[group, ctx],
                send_sem=send_sem.at[step],
                recv_sem=recv_sem.at[step],
                device_id={"ctx": target},
                device_id_type=MESH_ID,
            )
        )
        sends[-1].start()
    relays = [
        pltpu.make_async_remote_copy(
            src_ref=packed.at[ctx],
            dst_ref=kv.at[group, ctx],
            send_sem=relay_send.at[0],
            recv_sem=relay_recv.at[0],
            device_id={"group": 1 - group},
            device_id_type=MESH_ID,
        )
    ]
    relays[0].start()
    rows = embed[...].astype(jnp.float32)
    ss_out[...] = jnp.broadcast_to(jnp.sum(rows * rows, 1, keepdims=True), ss_out.shape)
    squares = pltpu.make_async_remote_copy(
        src_ref=ss_out,
        dst_ref=ss_in,
        send_sem=mp_send.at[0],
        recv_sem=mp_recv.at[0],
        device_id={"mp": 1 - mp},
        device_id_type=MESH_ID,
    )
    squares.start()
    squares.wait()
    square_sum = (ss_out[...] + ss_in[...])[:, :1]
    normal = (
        rows * lax.rsqrt(square_sum / D + 1e-05) * gain[...].astype(jnp.float32)
    ).astype(jnp.bfloat16)
    for slot in range(3):
        loads[slot].wait()
        part_out[slot] = jnp.dot(normal, wbuf[slot], preferred_element_type=jnp.float32)
    parts = pltpu.make_async_remote_copy(
        src_ref=part_out,
        dst_ref=part_in,
        send_sem=mp_send.at[1],
        recv_sem=mp_recv.at[1],
        device_id={"mp": 1 - mp},
        device_id_type=MESH_ID,
    )
    parts.start()
    for slot in range(3):
        loads[slot + 3].wait()
        table[slot] = jnp.dot(normal, wbuf[slot + 3], preferred_element_type=jnp.float32)
    parts.wait()
    shift = WINDOW - (ctx * span - first)
    for slot in range(3):
        table[slot] = pltpu.roll(table[slot] + part_in[slot], lax.rem(shift, WINDOW), 1)
    for step in range(1, count):
        source = lax.rem(ctx + count - step, count)
        sends[step - 1].wait_recv()
        relays.append(
            pltpu.make_async_remote_copy(
                src_ref=kv.at[group, source],
                dst_ref=kv.at[group, source],
                send_sem=relay_send.at[step],
                recv_sem=relay_recv.at[step],
                device_id={"group": 1 - group},
                device_id_type=MESH_ID,
            )
        )
        relays[-1].start()
    mine.wait()
    for step in range(1, count):
        sends[step - 1].wait_send()
    for relay in relays:
        relay.wait()


def exchange(packed, embed, gain, wq, wk, wv):
    count = packed.shape[0]
    vocab, features = embed.shape
    vmem = pl.BlockSpec(memory_space=pltpu.VMEM)
    anywhere = pl.BlockSpec(memory_space=pl.ANY)
    return pl.pallas_call(
        exchange_kernel,
        out_shape=(
            jax.ShapeDtypeStruct((2,) + packed.shape, jnp.bfloat16),
            jax.ShapeDtypeStruct((3, vocab, WINDOW), jnp.float32),
        ),
        in_specs=[anywhere, vmem, vmem, anywhere, anywhere, anywhere],
        out_specs=(anywhere, vmem),
        scratch_shapes=[
            pltpu.VMEM((6, features, WINDOW), jnp.bfloat16),
            pltpu.VMEM((vocab, 128), jnp.float32),
            pltpu.VMEM((vocab, 128), jnp.float32),
            pltpu.VMEM((3, vocab, WINDOW), jnp.float32),
            pltpu.VMEM((3, vocab, WINDOW), jnp.float32),
            pltpu.SemaphoreType.DMA((6,)),
            pltpu.SemaphoreType.DMA,
            pltpu.SemaphoreType.DMA((count,)),
            pltpu.SemaphoreType.DMA((count,)),
            pltpu.SemaphoreType.DMA((count,)),
            pltpu.SemaphoreType.DMA((count,)),
            pltpu.SemaphoreType.DMA((2,)),
            pltpu.SemaphoreType.DMA((2,)),
        ],
        compiler_params=pltpu.CompilerParams(collective_id=0, has_side_effects=True),
        name="exchange",
    )(packed, embed, gain, wq, wk, wv)


def attention_kernel(query, own_key, own_value, span_key, span_value, kv, bias, out, scores):
    row_block, width = query.shape
    count, keep = kv.shape[1], kv.shape[3]
    span_rows = span_key.shape[0]
    start = pl.program_id(0) * row_block
    decoding = lax.axis_index("group") == 1
    scale = 1.0 / math.sqrt(HD)
    across = (((1,), (1,)), ((), ()))
    row = lax.broadcasted_iota(jnp.int32, (row_block, span_rows), 0) + start
    col = lax.broadcasted_iota(jnp.int32, (row_block, span_rows), 1)
    limit = jnp.where(decoding, span_rows, row)
    own_row = lax.broadcasted_iota(jnp.int32, (row_block, row_block), 0)
    own_col = lax.broadcasted_iota(jnp.int32, (row_block, row_block), 1)
    own_limit = jnp.where(decoding, own_row, -1)
    own_seen = (own_row // STEPS == own_col // STEPS) & (own_col <= own_limit)
    lane = lax.broadcasted_iota(jnp.int32, (row_block, width), 1)
    result = None
    span_at = count * keep
    own_at = span_at + span_rows
    total = own_at + row_block
    for head in range(width // HD):
        inside = (lane >= head * HD) & (lane < (head + 1) * HD)
        head_query = jnp.where(inside, query[...], jnp.zeros_like(query[...]))
        for block in range(count):
            part = jnp.dot(head_query, kv[0, block, :width, :], preferred_element_type=jnp.float32)
            scores[:, block * keep : (block + 1) * keep] = part + bias[block]
        part = lax.dot_general(
            head_query, span_key[...], across, preferred_element_type=jnp.float32
        )
        scores[:, span_at:own_at] = jnp.where(col <= limit, part, -1e30)
        part = lax.dot_general(
            head_query, own_key[...], across, preferred_element_type=jnp.float32
        )
        scores[:, own_at:total] = jnp.where(own_seen, part, -1e30)
        top = jnp.max(scores[...], 1, keepdims=True)
        norm = jnp.zeros((row_block, 1), jnp.float32)
        acc = jnp.zeros((row_block, width), jnp.float32)
        for block in range(count):
            weights = jnp.exp((scores[:, block * keep : (block + 1) * keep] - top) * scale)
            norm += jnp.sum(weights, 1, keepdims=True)
            acc += lax.dot_general(
                weights.astype(jnp.bfloat16),
                kv[1, block, :width, :],
                across,
                preferred_element_type=jnp.float32,
            )
        for at, end, values in ((span_at, own_at, span_value), (own_at, total, own_value)):
            weights = jnp.exp((scores[:, at:end] - top) * scale)
            norm += jnp.sum(weights, 1, keepdims=True)
            acc += jnp.dot(
                weights.astype(jnp.bfloat16), values[...], preferred_element_type=jnp.float32
            )
        head_out = acc / norm
        result = head_out if result is None else jnp.where(inside, head_out, result)
    padded = jnp.concatenate(
        [result, jnp.zeros((row_block, -width % 128), jnp.float32)], 1
    )
    out[...] = jnp.transpose(padded)[:width].astype(jnp.bfloat16)[None]


def attention(query, own_key, own_value, span_key, span_value, kv, bias, row_block):
    rows, width = query.shape
    span_rows = span_key.shape[0]
    blocks = rows // row_block
    keys = kv.shape[1] * kv.shape[3] + span_rows + row_block
    by_rows = pl.BlockSpec((row_block, width), lambda i: (i, 0))
    whole = pl.BlockSpec((span_rows, width), lambda i: (0, 0))
    return pl.pallas_call(
        attention_kernel,
        grid=(blocks,),
        out_shape=jax.ShapeDtypeStruct((blocks, width, row_block), jnp.bfloat16),
        in_specs=[
            by_rows,
            by_rows,
            by_rows,
            whole,
            whole,
            pl.BlockSpec(kv.shape, lambda i: (0, 0, 0, 0)),
            pl.BlockSpec(bias.shape, lambda i: (0, 0, 0)),
        ],
        out_specs=pl.BlockSpec((1, width, row_block), lambda i: (i, 0, 0)),
        scratch_shapes=[pltpu.VMEM((row_block, keys), jnp.float32)],
        compiler_params=pltpu.CompilerParams(vmem_limit_bytes=56 << 20),
        name="attention",
    )(query, own_key, own_value, span_key, span_value, kv, bias)


def give_back_kernel(parts, got, own_sem, send_sem, recv_sem):
    count = parts.shape[0]
    ctx = lax.axis_index("ctx")
    barrier = pltpu.get_barrier_semaphore()
    for step in range(1, count):
        pl.semaphore_signal(
            barrier, inc=1, device_id={"ctx": lax.rem(ctx + step, count)}, device_id_type=MESH_ID
        )
    mine = pltpu.make_async_copy(parts.at[ctx], got.at[ctx], own_sem)
    mine.start()
    pl.semaphore_wait(barrier, count - 1)
    sends = []
    for step in range(1, count):
        target = lax.rem(ctx + step, count)
        sends.append(
            pltpu.make_async_remote_copy(
                src_ref=parts.at[target],
                dst_ref=got.at[ctx],
                send_sem=send_sem.at[step],
                recv_sem=recv_sem.at[step],
                device_id={"ctx": target},
                device_id_type=MESH_ID,
            )
        )
        sends[-1].start()
    mine.wait()
    for send in sends:
        send.wait()


def give_back(parts):
    count = parts.shape[0]
    anywhere = pl.BlockSpec(memory_space=pl.ANY)
    return pl.pallas_call(
        give_back_kernel,
        out_shape=jax.ShapeDtypeStruct(parts.shape, parts.dtype),
        in_specs=[anywhere],
        out_specs=anywhere,
        scratch_shapes=[
            pltpu.SemaphoreType.DMA,
            pltpu.SemaphoreType.DMA((count,)),
            pltpu.SemaphoreType.DMA((count,)),
        ],
        compiler_params=pltpu.CompilerParams(collective_id=1, has_side_effects=True),
        name="give_back",
    )(parts)


def split_three(values):
    high = lax.reduce_precision(values, 8, 7)
    rest = values - high
    middle = lax.reduce_precision(rest, 8, 7)
    return jnp.concatenate([high, middle, rest - middle], 0).astype(jnp.bfloat16)


def partner(table):
    pieces = table.reshape(table.shape[0], -1, 2, 2, HD // 4)
    swapped = jnp.stack([-pieces[:, :, :, 1], pieces[:, :, :, 0]], 3)
    return swapped.reshape(table.shape)


def rotation(positions, width):
    quarter = HD // 4
    lane = jnp.arange(width) % HD
    frequency = 10000.0 ** (-(lane % quarter).astype(jnp.float32) / quarter)
    column = (positions % PROT).astype(jnp.float32)
    homolog = (positions // PROT).astype(jnp.float32)
    angles = jnp.where(lane[None] < HD // 2, column[:, None], homolog[:, None]) * frequency[None]
    return jnp.cos(angles), jnp.sin(angles)


def by_heads(
    token_ids,
    span_offset,
    shard_lengths,
    embed_table,
    norm_gain,
    query_weight,
    key_weight,
    value_weight,
    cache_keys,
    cache_values,
):
    row_count = token_ids.shape[1]
    count = lax.axis_size("ctx")
    rows = row_count * count
    cache_count, local_width = cache_keys.shape
    width = local_width // count
    vocab = embed_table.shape[0]
    decoding = lax.axis_index("group") == 1
    mine = jnp.where(decoding, cache_values, cache_keys).T.reshape(count, width, cache_count)
    meta = jnp.zeros((META, cache_count), jnp.int32)
    meta = meta.at[0, :row_count].set(token_ids[0])
    meta = meta.at[1].set(shard_lengths[0] // 16).at[2].set(shard_lengths[0] % 16)
    meta = jnp.broadcast_to(meta.astype(jnp.bfloat16)[None], (count, META, cache_count))
    packed = jnp.concatenate([mine, meta], 1)
    kv, table = exchange(
        packed, embed_table, norm_gain[None], query_weight, key_weight, value_weight
    )
    tokens = kv[:, :, width, :row_count].astype(jnp.int32).reshape(2, rows)
    length = kv[0, :, width + 1 : width + 3, 0].astype(jnp.int32)
    length = length[:, 0] * 16 + length[:, 1]
    slot = jnp.arange(cache_count, dtype=jnp.int32)
    bias = jnp.where(slot[None] < length[:, None], 0.0, -1e30).astype(jnp.float32)[:, None]
    tables = table[:, :, :width]
    query_table, key_table, value_table = tables[0], tables[1], tables[2]
    key_tables = [key_table, partner(key_table), value_table]
    span_tables = split_three(jnp.concatenate(key_tables, 1))
    own_tables = split_three(
        jnp.concatenate(key_tables + [query_table, partner(query_table)], 1)
    )

    def pick(tokens_in, tables_in):
        hot = (tokens_in[:, None] == jnp.arange(3 * vocab, dtype=jnp.int32)[None] % vocab)
        return jnp.dot(hot.astype(jnp.bfloat16), tables_in, preferred_element_type=jnp.float32)

    index = jnp.arange(rows, dtype=jnp.int32)
    span_cos, span_sin = rotation(span_offset[0] + index, width)
    step_cos, step_sin = rotation(
        span_offset[0] + rows + jnp.arange(8, dtype=jnp.int32) % STEPS, width
    )
    own_cos = jnp.where(decoding, jnp.tile(step_cos, (rows // 8, 1)), span_cos)
    own_sin = jnp.where(decoding, jnp.tile(step_sin, (rows // 8, 1)), span_sin)
    span = pick(tokens[0], span_tables)
    own = pick(jnp.where(decoding, tokens[1], tokens[0]), own_tables)
    span_key = (span[:, :width] * span_cos + span[:, width : 2 * width] * span_sin)
    own_key = (own[:, :width] * own_cos + own[:, width : 2 * width] * own_sin)
    query = own[:, 3 * width : 4 * width] * own_cos + own[:, 4 * width :] * own_sin
    span_value = span[:, 2 * width :]
    own_value = own[:, 2 * width : 3 * width]
    out = attention(
        query.astype(jnp.bfloat16),
        own_key.astype(jnp.bfloat16),
        own_value.astype(jnp.bfloat16),
        span_key.astype(jnp.bfloat16),
        span_value.astype(jnp.bfloat16),
        kv,
        bias,
        row_count,
    )
    return give_back(out).reshape(local_width, row_count).T[None]


def solution(mesh):
    placed = (
        P("group", "ctx"),
        P(),
        P("ctx"),
        P(None, "mp"),
        P("mp"),
        P("mp", None),
        P("mp", None),
        P("mp", None),
        P("ctx", "mp"),
        P("ctx", "mp"),
    )
    heads = D // HD // mesh.shape["mp"]
    body = by_heads if heads == 2 * mesh.shape["ctx"] else local
    return jax.shard_map(
        body, mesh=mesh, in_specs=placed, out_specs=P("group", "ctx", "mp"), check_vma=False
    )
```

```python
import math

import jax
import jax.numpy as jnp
from jax import lax
from jax.experimental import pallas as pl
from jax.experimental.pallas import tpu as pltpu
from jax.sharding import PartitionSpec as P

D = 2560
HD = 80
PROT = 256
STEPS = 4


def passed_along(value, axis, steps):
    count = lax.axis_size(axis)
    first, last = (max(0, -steps), min(count, count - steps))
    return lax.ppermute(value, axis, [(source, source + steps) for source in range(first, last)])


def rotate(values_in, positions):
    row_count = values_in.shape[0]
    head_count = values_in.shape[1] // HD
    quarter = HD // 4
    column = (positions % PROT).astype(jnp.float32)
    homolog = (positions // PROT).astype(jnp.float32)
    frequency = 10000.0 ** (-jnp.arange(quarter, dtype=jnp.float32) / quarter)
    angles = jnp.stack([column[:, None] * frequency, homolog[:, None] * frequency], 1)
    cosine = jnp.cos(angles)[:, None, :, None, :]
    sine_table = jnp.sin(angles)[:, None, :, None, :]
    pieces = values_in.reshape(row_count, head_count, 2, 2, quarter)
    partner = jnp.stack([-pieces[:, :, :, 1], pieces[:, :, :, 0]], 3)
    return (pieces * cosine + partner * sine_table).reshape(row_count, head_count * HD)


def block_partial(
    query_block, start, all_keys, all_values, live_length, span_base, cache_count, decoding
):
    block_rows = query_block.shape[0]
    head_count = query_block.shape[1] // HD
    key_slots = all_keys.shape[0]
    query_heads = query_block.reshape(block_rows, head_count, HD)
    key_heads = all_keys.reshape(key_slots, head_count, HD)
    value_heads = all_values.reshape(key_slots, head_count, HD)
    scores = jnp.einsum(
        "qhd,khd->hqk", query_heads, key_heads, preferred_element_type=jnp.float32
    ) * (1.0 / math.sqrt(HD))
    slot = jnp.arange(key_slots, dtype=jnp.int32)
    query_index = start + jnp.arange(block_rows, dtype=jnp.int32)
    cache_live = (slot < cache_count) & (slot < live_length)
    span_index = span_base + slot - cache_count
    span_seen = (slot >= cache_count)[None, :] & (
        decoding | (span_index[None, :] <= query_index[:, None])
    )
    visible = (cache_live[None, :] | span_seen)[None]
    block_max = jnp.max(jnp.where(visible, scores, -1e30), -1)
    weights = jnp.where(visible, jnp.exp(scores - block_max[..., None]), 0.0)
    block_sum = jnp.sum(weights, -1)
    block_acc = jnp.einsum(
        "hqk,khd->qhd",
        weights.astype(jnp.bfloat16),
        value_heads,
        preferred_element_type=jnp.float32,
    )
    return (block_max.T, block_sum.T, block_acc.reshape(block_rows, head_count * HD))


def local(
    token_ids,
    span_offset,
    shard_lengths,
    embed_table,
    norm_gain,
    query_weight,
    key_weight,
    value_weight,
    cache_keys,
    cache_values,
):
    token_row = token_ids[0]
    row_count = token_row.shape[0]
    ctx_count = lax.axis_size("ctx")
    ctx_index = lax.axis_index("ctx")
    decoding = lax.axis_index("group") == 1
    one_hot = (
        token_row[:, None] == jnp.arange(embed_table.shape[0], dtype=jnp.int32)[None, :]
    ).astype(jnp.bfloat16)
    embedded = jnp.dot(one_hot, embed_table, preferred_element_type=jnp.float32)
    square_sum = lax.psum(jnp.sum(embedded * embedded, 1), "mp")
    normal_rows = (
        embedded * lax.rsqrt(square_sum / D + 1e-05)[:, None] * norm_gain.astype(jnp.float32)
    ).astype(jnp.bfloat16)
    query_part = jnp.dot(normal_rows, query_weight, preferred_element_type=jnp.float32)
    key_part = jnp.dot(normal_rows, key_weight, preferred_element_type=jnp.float32)
    value_part = jnp.dot(normal_rows, value_weight, preferred_element_type=jnp.float32)
    query_full, key_full, value_full = (
        lax.psum_scatter(query_part, "mp", scatter_dimension=1, tiled=True),
        lax.psum_scatter(key_part, "mp", scatter_dimension=1, tiled=True),
        lax.psum_scatter(value_part, "mp", scatter_dimension=1, tiled=True),
    )
    offset_value = span_offset[0]
    local_iota = jnp.arange(row_count, dtype=jnp.int32)
    positions = jnp.where(
        decoding,
        offset_value + row_count * ctx_count + local_iota % STEPS,
        offset_value + ctx_index * row_count + local_iota,
    )
    queries = rotate(query_full, positions).astype(jnp.bfloat16)
    new_keys = rotate(key_full, positions).astype(jnp.bfloat16)
    new_values = value_full.astype(jnp.bfloat16)
    width = queries.shape[1]
    head_count = width // HD
    span_keys, span_values = passed_along((new_keys, new_values), "group", 1)
    block_keys = jnp.where(decoding, span_keys, new_keys)
    block_values = jnp.where(decoding, span_values, new_values)
    cache_count = cache_keys.shape[0]
    all_keys = jnp.concatenate([cache_keys, block_keys], 0)
    all_values = jnp.concatenate([cache_values, block_values], 0)
    live_length = shard_lengths[0]
    span_base = ctx_index * row_count
    gathered = lax.all_gather(queries, "ctx", axis=0, tiled=True)
    total = gathered.shape[0]
    block_rows = math.gcd(total, 512)
    block_count = total // block_rows
    block_starts = jnp.arange(block_count, dtype=jnp.int32) * block_rows

    def one_block(pair):
        return block_partial(
            pair[0], pair[1], all_keys, all_values, live_length, span_base, cache_count, decoding
        )

    maxima, totals, sums = lax.map(
        one_block, (gathered.reshape(block_count, block_rows, width), block_starts)
    )
    maxima = maxima.reshape(total, head_count)
    totals = totals.reshape(total, head_count)
    sums = sums.reshape(total, width)
    got_max, got_sum, got_acc = (
        lax.all_to_all(maxima[None], "ctx", split_axis=1, concat_axis=0, tiled=True),
        lax.all_to_all(totals[None], "ctx", split_axis=1, concat_axis=0, tiled=True),
        lax.all_to_all(sums[None], "ctx", split_axis=1, concat_axis=0, tiled=True),
    )
    whole_max = jnp.max(got_max, 0)
    rescale = jnp.exp(got_max - whole_max[None])
    whole_sum = jnp.sum(rescale * got_sum, 0)
    whole_acc = jnp.sum(got_acc * jnp.repeat(rescale, HD, axis=2), 0)
    cands = row_count // STEPS
    own_q = queries.reshape(cands, STEPS, head_count, HD)
    own_k = new_keys.reshape(cands, STEPS, head_count, HD)
    own_v = new_values.reshape(cands, STEPS, head_count, HD)
    own_scores = jnp.einsum("ashd,athd->ahst", own_q, own_k, preferred_element_type=jnp.float32) * (
        1.0 / math.sqrt(HD)
    )
    step_iota = jnp.arange(STEPS, dtype=jnp.int32)
    own_visible = (step_iota[None, :] <= step_iota[:, None]) & decoding
    own_max = jnp.max(jnp.where(own_visible, own_scores, -1e30), -1)
    final_max = jnp.maximum(whole_max, own_max.transpose(0, 2, 1).reshape(row_count, head_count))
    keep_old = jnp.exp(whole_max - final_max)
    final_cand = final_max.reshape(cands, STEPS, head_count).transpose(0, 2, 1)
    own_weights = jnp.where(own_visible, jnp.exp(own_scores - final_cand[..., None]), 0.0)
    own_sum = jnp.sum(own_weights, -1).transpose(0, 2, 1).reshape(row_count, head_count)
    own_acc = jnp.einsum(
        "ahst,athd->ashd",
        own_weights.astype(jnp.bfloat16),
        own_v,
        preferred_element_type=jnp.float32,
    ).reshape(row_count, width)
    numer = whole_acc * jnp.repeat(keep_old, HD, axis=1) + own_acc
    denom = whole_sum * keep_old + own_sum
    output = numer / jnp.repeat(denom, HD, axis=1)
    return output.astype(jnp.bfloat16)[None]


MESH_ID = pl.DeviceIdType.MESH
WINDOW = 256
ROW_BLOCK = 256
HIDDEN = -1e30


def flipped(index, mask):
    result = index
    bit = 1
    while bit <= mask:
        if mask & bit:
            result = result + bit * (1 - 2 * (index // bit % 2))
        bit *= 2
    return result


def masked_weights(scores, top):
    return jnp.exp2((scores - top) * (math.log2(math.e) / math.sqrt(HD)))


def across(left, right):
    return lax.dot_general(
        left, right, (((1,), (1,)), ((), ())), preferred_element_type=jnp.float32
    )


def layer_kernel(
    offset, packed, note, embed, gain, frequency, wq, wk, wv, got,
    kv, notes, wbuf, ss_out, ss_in, part_out, part_in, table, cosine, sine, query, own_key,
    own_value, span_key, span_value, first_max, first_sum, first_acc, scores, bias, out_parts,
    wsem, own_sem, note_send, note_recv, send_sem, recv_sem, relay_send, relay_recv, mp_send,
    mp_recv, out_send, out_recv, out_own,
):
    count, width, keep = packed.shape
    row_count = note.shape[1]
    rows = row_count * count
    vocab = embed.shape[0]
    group, ctx, mp = lax.axis_index("group"), lax.axis_index("ctx"), lax.axis_index("mp")
    decoding = group == 1
    half = wq.shape[1] // 2
    first = pl.multiple_of(ctx * width // 128 * 128, 128)
    far_first = sorted(range(1, count), key=lambda mask: -mask)
    barrier = pltpu.get_barrier_semaphore()
    for mask in far_first:
        for side in (group, 1 - group):
            pl.semaphore_signal(
                barrier,
                inc=1,
                device_id={"ctx": flipped(ctx, mask), "group": side},
                device_id_type=MESH_ID,
            )
    pl.semaphore_signal(barrier, inc=1, device_id={"group": 1 - group}, device_id_type=MESH_ID)
    pl.semaphore_signal(barrier, inc=1, device_id={"mp": 1 - mp}, device_id_type=MESH_ID)
    loads = []
    for slot in range(6):
        side = 1 - mp if slot < 3 else mp
        weight = (wq, wk, wv)[slot % 3]
        column = pl.multiple_of(side * half + first, 128)
        loads.append(
            pltpu.make_async_copy(
                weight.at[:, pl.ds(column, WINDOW)], wbuf.at[slot], wsem.at[slot]
            )
        )
        loads[-1].start()
    mine = pltpu.make_async_copy(packed.at[ctx], kv.at[group, ctx], own_sem.at[0])
    mine.start()
    my_note = pltpu.make_async_copy(note, notes.at[group, ctx], own_sem.at[1])
    my_note.start()
    embedded = embed[...].astype(jnp.float32)
    ss_out[...] = jnp.broadcast_to(jnp.sum(embedded * embedded, 1, keepdims=True), ss_out.shape)
    pl.semaphore_wait(barrier, 2 * count)
    squares = pltpu.make_async_remote_copy(
        src_ref=ss_out,
        dst_ref=ss_in,
        send_sem=mp_send.at[0],
        recv_sem=mp_recv.at[0],
        device_id={"mp": 1 - mp},
        device_id_type=MESH_ID,
    )
    squares.start()
    note_copies = []
    for mask in range(count):
        for same in (True, False):
            if mask == 0 and same:
                continue
            slot = 2 * mask + (0 if same else 1)
            note_copies.append(
                pltpu.make_async_remote_copy(
                    src_ref=note,
                    dst_ref=notes.at[group, ctx],
                    send_sem=note_send.at[slot],
                    recv_sem=note_recv.at[slot],
                    device_id={
                        "ctx": flipped(ctx, mask),
                        "group": group if same else 1 - group,
                    },
                    device_id_type=MESH_ID,
                )
            )
            note_copies[-1].start()
    sends = {}
    for mask in far_first:
        target = flipped(ctx, mask)
        sends[mask] = pltpu.make_async_remote_copy(
            src_ref=packed.at[target],
            dst_ref=kv.at[group, ctx],
            send_sem=send_sem.at[mask],
            recv_sem=recv_sem.at[mask],
            device_id={"ctx": target},
            device_id_type=MESH_ID,
        )
        sends[mask].start()
    relays = [
        pltpu.make_async_remote_copy(
            src_ref=packed.at[ctx],
            dst_ref=kv.at[group, ctx],
            send_sem=relay_send.at[0],
            recv_sem=relay_recv.at[0],
            device_id={"group": 1 - group},
            device_id_type=MESH_ID,
        )
    ]
    relays[0].start()

    def relay(mask):
        source = flipped(ctx, mask)
        sends[mask].wait_recv()
        relays.append(
            pltpu.make_async_remote_copy(
                src_ref=kv.at[group, source],
                dst_ref=kv.at[group, source],
                send_sem=relay_send.at[mask],
                recv_sem=relay_recv.at[mask],
                device_id={"group": 1 - group},
                device_id_type=MESH_ID,
            )
        )
        relays[-1].start()

    squares.wait()
    square_sum = (ss_out[...] + ss_in[...])[:, :1]
    normal = (
        embedded * lax.rsqrt(square_sum / D + 1e-05) * gain[...].astype(jnp.float32)
    ).astype(jnp.bfloat16)
    for slot in range(3):
        loads[slot].wait()
        part_out[slot] = jnp.dot(normal, wbuf[slot], preferred_element_type=jnp.float32)
    parts = pltpu.make_async_remote_copy(
        src_ref=part_out,
        dst_ref=part_in,
        send_sem=mp_send.at[1],
        recv_sem=mp_recv.at[1],
        device_id={"mp": 1 - mp},
        device_id_type=MESH_ID,
    )
    parts.start()
    for slot in range(3):
        loads[slot + 3].wait()
        table[slot] = jnp.dot(normal, wbuf[slot + 3], preferred_element_type=jnp.float32)

    @pl.loop(0, rows // row_count + 1)
    def _(block):
        index = lax.broadcasted_iota(jnp.int32, (row_count, width), 0)
        lane = lax.broadcasted_iota(jnp.int32, (row_count, width), 1)
        last = block == rows // row_count
        at = pl.multiple_of(block * row_count, row_count)
        position = offset[0] + at + jnp.where(last, index % STEPS, index)
        second = lane % HD >= HD // 2
        angle = jnp.where(second, position // PROT, position % PROT).astype(
            jnp.float32
        ) * frequency[...]
        cosine[pl.ds(at, row_count)] = jnp.cos(angle)
        sine[pl.ds(at, row_count)] = jnp.sin(angle)

    my_note.wait()
    for copy in note_copies:
        copy.wait()
    for source in range(count):
        length = notes[0, source, 1:2, :]
        for at in range(0, keep, 128):
            slot = lax.broadcasted_iota(jnp.int32, (1, 128), 1) + at
            bias[source : source + 1, at : at + 128] = jnp.where(slot < length, 0.0, HIDDEN)
    parts.wait()
    shift = lax.rem(WINDOW - (ctx * width - first), WINDOW)
    lane = lax.broadcasted_iota(jnp.int32, (vocab, WINDOW), 1)
    even = lane % (HD // 2) < HD // 4
    tables = []
    for slot in range(3):
        whole = pltpu.roll(table[slot] + part_in[slot], shift, 1)
        tables.append(whole)
        if slot < 2:
            tables.append(
                jnp.where(
                    even,
                    -pltpu.roll(whole, WINDOW - HD // 4, 1),
                    pltpu.roll(whole, HD // 4, 1),
                )
            )
    splits = []
    for whole in tables:
        high = whole.astype(jnp.bfloat16)
        rest = whole - high.astype(jnp.float32)
        middle = rest.astype(jnp.bfloat16)
        low = (rest - middle.astype(jnp.float32)).astype(jnp.bfloat16)
        splits.append((high, middle, low))

    def picked(hot, split):
        total = None
        for part in split:
            term = jnp.dot(hot, part, preferred_element_type=jnp.float32)
            total = term if total is None else total + term
        return total[:, :width]

    def hot_rows(token_line):
        letter = lax.broadcasted_iota(jnp.int32, (vocab, row_count), 0)
        hot = (letter == token_line).astype(jnp.float32)
        return jnp.transpose(hot).astype(jnp.bfloat16)

    value_table = splits[4][:1]
    for block in range(count):
        here = slice(block * row_count, (block + 1) * row_count)
        cos, sin = cosine[here], sine[here]
        step_cos, step_sin = cosine[rows:], sine[rows:]
        hot = hot_rows(notes[0, block, 0:1, :])
        span_key[here] = (
            picked(hot, splits[2]) * cos + picked(hot, splits[3]) * sin
        ).astype(jnp.bfloat16)
        span_value[here] = picked(hot, value_table).astype(jnp.bfloat16)
        own_cos = jnp.where(decoding, step_cos, cos)
        own_sin = jnp.where(decoding, step_sin, sin)
        hot = hot_rows(jnp.where(decoding, notes[1, block, 0:1, :], notes[0, block, 0:1, :]))
        query[here] = (
            picked(hot, splits[0]) * own_cos + picked(hot, splits[1]) * own_sin
        ).astype(jnp.bfloat16)
        own_key[here] = (
            picked(hot, splits[2]) * own_cos + picked(hot, splits[3]) * own_sin
        ).astype(jnp.bfloat16)
        own_value[here] = picked(hot, value_table).astype(jnp.bfloat16)

    heads = width // HD
    head_lane = lax.broadcasted_iota(jnp.int32, (ROW_BLOCK, width), 1)
    inside = [(head_lane >= head * HD) & (head_lane < (head + 1) * HD) for head in range(heads)]

    def one_head(block_query, head):
        return jnp.where(inside[head], block_query, jnp.zeros_like(block_query))

    row = lax.broadcasted_iota(jnp.int32, (ROW_BLOCK, rows), 0)
    col = lax.broadcasted_iota(jnp.int32, (ROW_BLOCK, rows), 1)
    own_row = lax.broadcasted_iota(jnp.int32, (ROW_BLOCK, ROW_BLOCK), 0)
    own_col = lax.broadcasted_iota(jnp.int32, (ROW_BLOCK, ROW_BLOCK), 1)
    own_limit = jnp.where(decoding, own_row, -1)
    own_seen = (own_row // STEPS == own_col // STEPS) & (own_col <= own_limit)
    blocks = rows // ROW_BLOCK
    pending = list(far_first)
    for block in range(blocks):
        here = slice(block * ROW_BLOCK, (block + 1) * ROW_BLOCK)
        limit = jnp.where(decoding, rows, row + block * ROW_BLOCK)
        tops, sums, accs = None, None, None
        for head in range(heads):
            head_query = one_head(query[here], head)
            span_scores = jnp.where(col <= limit, across(head_query, span_key[...]), HIDDEN)
            own_scores = jnp.where(own_seen, across(head_query, own_key[here]), HIDDEN)
            top = jnp.maximum(
                jnp.max(span_scores, 1, keepdims=True), jnp.max(own_scores, 1, keepdims=True)
            )
            span_weights = masked_weights(span_scores, top)
            own_weights = masked_weights(own_scores, top)
            total = jnp.sum(span_weights, 1, keepdims=True) + jnp.sum(
                own_weights, 1, keepdims=True
            )
            acc = jnp.dot(
                span_weights.astype(jnp.bfloat16), span_value[...],
                preferred_element_type=jnp.float32,
            ) + jnp.dot(
                own_weights.astype(jnp.bfloat16), own_value[here],
                preferred_element_type=jnp.float32,
            )
            if head == 0:
                tops, sums, accs = top, total, acc
            else:
                tops = jnp.where(inside[head], top, tops)
                sums = jnp.where(inside[head], total, sums)
                accs = jnp.where(inside[head], acc, accs)
        first_max[here], first_sum[here], first_acc[here] = tops, sums, accs
        for _ in range(-(-(count - 1) // blocks)):
            if pending:
                relay(pending.pop(0))
    mine.wait()
    for copy in relays:
        copy.wait()
    for mask in far_first:
        sends[mask].wait_send()

    per_block = ROW_BLOCK // row_count

    def out_copy(owner):
        return pltpu.make_async_remote_copy(
            src_ref=out_parts.at[owner],
            dst_ref=got.at[ctx],
            send_sem=out_send.at[owner],
            recv_sem=out_recv.at[ctx],
            device_id={"ctx": owner},
            device_id_type=MESH_ID,
        )

    @pl.loop(0, blocks)
    def _(turn):
        block = lax.rem(ctx // per_block + 1 + turn, blocks)
        at = pl.multiple_of(block * ROW_BLOCK, ROW_BLOCK)
        here = pl.ds(at, ROW_BLOCK)
        block_query = query[here, :]
        old_top, old_sum, old_acc = first_max[here, :], first_sum[here, :], first_acc[here, :]
        result = None
        for head in range(heads):
            head_query = one_head(block_query, head)
            for source in range(count):
                part = jnp.dot(head_query, kv[0, source], preferred_element_type=jnp.float32)
                scores[:, source * keep : (source + 1) * keep] = part + bias[source : source + 1]
            before = old_top[:, head * HD : head * HD + 1]
            top = jnp.maximum(jnp.max(scores[...], 1, keepdims=True), before)
            ratio = masked_weights(before, top)
            total = old_sum[:, head * HD : head * HD + 1] * ratio
            acc = old_acc * ratio
            for source in range(count):
                weights = masked_weights(scores[:, source * keep : (source + 1) * keep], top)
                total += jnp.sum(weights, 1, keepdims=True)
                acc += across(weights.astype(jnp.bfloat16), kv[1, source])
            head_out = acc / total
            result = head_out if head == 0 else jnp.where(inside[head], head_out, result)
        padded = jnp.concatenate(
            [result, jnp.zeros((ROW_BLOCK, -width % 128), jnp.float32)], 1
        )
        turned = jnp.transpose(padded)[:width].astype(jnp.bfloat16)
        for piece in range(per_block):
            owner = block * per_block + piece
            out_parts[owner] = turned[:, piece * row_count : (piece + 1) * row_count]

            @pl.when(owner != ctx)
            def _():
                out_copy(owner).start()

            @pl.when(owner == ctx)
            def _():
                pltpu.make_async_copy(out_parts.at[ctx], got.at[ctx], out_own).start()

    pltpu.make_async_copy(out_parts.at[ctx], got.at[ctx], out_own).wait()
    for mask in far_first:
        peer = flipped(ctx, mask)
        arrival = pltpu.make_async_remote_copy(
            src_ref=out_parts.at[peer],
            dst_ref=got.at[peer],
            send_sem=out_send.at[peer],
            recv_sem=out_recv.at[peer],
            device_id={"ctx": peer},
            device_id_type=MESH_ID,
        )
        arrival.wait()


def layer(offset, packed, note, embed, gain, frequency, wq, wk, wv):
    count, width, keep = packed.shape
    row_count = note.shape[1]
    rows = row_count * count
    vocab, features = embed.shape
    vmem = pl.BlockSpec(memory_space=pltpu.VMEM)
    anywhere = pl.BlockSpec(memory_space=pl.ANY)
    wide, narrow = jnp.float32, jnp.bfloat16
    dma = pltpu.SemaphoreType.DMA
    return pl.pallas_call(
        layer_kernel,
        out_shape=jax.ShapeDtypeStruct((count, width, row_count), narrow),
        in_specs=[pl.BlockSpec(memory_space=pltpu.SMEM), anywhere, vmem, vmem, vmem, vmem]
        + [anywhere] * 3,
        out_specs=vmem,
        scratch_shapes=[
            pltpu.VMEM((2, count, width, keep), narrow),
            pltpu.VMEM((2, count) + note.shape, jnp.int32),
            pltpu.VMEM((6, features, WINDOW), narrow),
            pltpu.VMEM((vocab, 128), wide),
            pltpu.VMEM((vocab, 128), wide),
            pltpu.VMEM((3, vocab, WINDOW), wide),
            pltpu.VMEM((3, vocab, WINDOW), wide),
            pltpu.VMEM((3, vocab, WINDOW), wide),
            pltpu.VMEM((rows + row_count, width), wide),
            pltpu.VMEM((rows + row_count, width), wide),
            pltpu.VMEM((rows, width), narrow),
            pltpu.VMEM((rows, width), narrow),
            pltpu.VMEM((rows, width), narrow),
            pltpu.VMEM((rows, width), narrow),
            pltpu.VMEM((rows, width), narrow),
            pltpu.VMEM((rows, width), wide),
            pltpu.VMEM((rows, width), wide),
            pltpu.VMEM((rows, width), wide),
            pltpu.VMEM((ROW_BLOCK, count * keep), wide),
            pltpu.VMEM((count, keep), wide),
            pltpu.VMEM((count, width, row_count), narrow),
            dma((6,)),
            dma((2,)),
            dma((2 * count,)),
            dma((2 * count,)),
            dma((count,)),
            dma((count,)),
            dma((count,)),
            dma((count,)),
            dma((2,)),
            dma((2,)),
            dma((count,)),
            dma((count,)),
            dma,
        ],
        compiler_params=pltpu.CompilerParams(
            collective_id=0, has_side_effects=True, vmem_limit_bytes=56 << 20
        ),
        name="layer",
    )(offset, packed, note, embed, gain, frequency, wq, wk, wv)


def by_heads(
    token_ids,
    span_offset,
    shard_lengths,
    embed_table,
    norm_gain,
    query_weight,
    key_weight,
    value_weight,
    cache_keys,
    cache_values,
):
    row_count = token_ids.shape[1]
    count = lax.axis_size("ctx")
    cache_count, local_width = cache_keys.shape
    width = local_width // count
    decoding = lax.axis_index("group") == 1
    packed = jnp.where(decoding, cache_values, cache_keys).T.reshape(count, width, cache_count)
    note = jnp.where(
        jnp.arange(8, dtype=jnp.int32)[:, None] == 0, token_ids, shard_lengths[:, None]
    )
    quarter = HD // 4
    frequency = 10000.0 ** (-jnp.arange(quarter, dtype=jnp.float32) / quarter)
    frequency = jnp.tile(frequency, width // quarter)[None]
    out = layer(
        span_offset, packed, note, embed_table, norm_gain[None], frequency,
        query_weight, key_weight, value_weight,
    )
    return out.reshape(local_width, row_count).T[None]


def solution(mesh):
    placed = (
        P("group", "ctx"),
        P(),
        P("ctx"),
        P(None, "mp"),
        P("mp"),
        P("mp", None),
        P("mp", None),
        P("mp", None),
        P("ctx", "mp"),
        P("ctx", "mp"),
    )
    heads = D // HD // mesh.shape["mp"]
    count = mesh.shape["ctx"]
    fits = heads == 2 * count and count & (count - 1) == 0
    body = by_heads if fits else local
    return jax.shard_map(
        body, mesh=mesh, in_specs=placed, out_specs=P("group", "ctx", "mp"), check_vma=False
    )
```

```python
import math

import jax
import jax.numpy as jnp
import numpy as np
from jax import lax
from jax.experimental import pallas as pl
from jax.experimental.pallas import tpu as pltpu
from jax.sharding import PartitionSpec as P

D = 2560
HD = 80
PROT = 256
STEPS = 4


def passed_along(value, axis, steps):
    count = lax.axis_size(axis)
    first, last = (max(0, -steps), min(count, count - steps))
    return lax.ppermute(value, axis, [(source, source + steps) for source in range(first, last)])


def rotate(values_in, positions):
    row_count = values_in.shape[0]
    head_count = values_in.shape[1] // HD
    quarter = HD // 4
    column = (positions % PROT).astype(jnp.float32)
    homolog = (positions // PROT).astype(jnp.float32)
    frequency = 10000.0 ** (-jnp.arange(quarter, dtype=jnp.float32) / quarter)
    angles = jnp.stack([column[:, None] * frequency, homolog[:, None] * frequency], 1)
    cosine = jnp.cos(angles)[:, None, :, None, :]
    sine_table = jnp.sin(angles)[:, None, :, None, :]
    pieces = values_in.reshape(row_count, head_count, 2, 2, quarter)
    partner = jnp.stack([-pieces[:, :, :, 1], pieces[:, :, :, 0]], 3)
    return (pieces * cosine + partner * sine_table).reshape(row_count, head_count * HD)


def block_partial(
    query_block, start, all_keys, all_values, live_length, span_base, cache_count, decoding
):
    block_rows = query_block.shape[0]
    head_count = query_block.shape[1] // HD
    key_slots = all_keys.shape[0]
    query_heads = query_block.reshape(block_rows, head_count, HD)
    key_heads = all_keys.reshape(key_slots, head_count, HD)
    value_heads = all_values.reshape(key_slots, head_count, HD)
    scores = jnp.einsum(
        "qhd,khd->hqk", query_heads, key_heads, preferred_element_type=jnp.float32
    ) * (1.0 / math.sqrt(HD))
    slot = jnp.arange(key_slots, dtype=jnp.int32)
    query_index = start + jnp.arange(block_rows, dtype=jnp.int32)
    cache_live = (slot < cache_count) & (slot < live_length)
    span_index = span_base + slot - cache_count
    span_seen = (slot >= cache_count)[None, :] & (
        decoding | (span_index[None, :] <= query_index[:, None])
    )
    visible = (cache_live[None, :] | span_seen)[None]
    block_max = jnp.max(jnp.where(visible, scores, -1e30), -1)
    weights = jnp.where(visible, jnp.exp(scores - block_max[..., None]), 0.0)
    block_sum = jnp.sum(weights, -1)
    block_acc = jnp.einsum(
        "hqk,khd->qhd",
        weights.astype(jnp.bfloat16),
        value_heads,
        preferred_element_type=jnp.float32,
    )
    return (block_max.T, block_sum.T, block_acc.reshape(block_rows, head_count * HD))


def local(
    token_ids,
    span_offset,
    shard_lengths,
    embed_table,
    norm_gain,
    query_weight,
    key_weight,
    value_weight,
    cache_keys,
    cache_values,
):
    token_row = token_ids[0]
    row_count = token_row.shape[0]
    ctx_count = lax.axis_size("ctx")
    ctx_index = lax.axis_index("ctx")
    decoding = lax.axis_index("group") == 1
    one_hot = (
        token_row[:, None] == jnp.arange(embed_table.shape[0], dtype=jnp.int32)[None, :]
    ).astype(jnp.bfloat16)
    embedded = jnp.dot(one_hot, embed_table, preferred_element_type=jnp.float32)
    square_sum = lax.psum(jnp.sum(embedded * embedded, 1), "mp")
    normal_rows = (
        embedded * lax.rsqrt(square_sum / D + 1e-05)[:, None] * norm_gain.astype(jnp.float32)
    ).astype(jnp.bfloat16)
    query_part = jnp.dot(normal_rows, query_weight, preferred_element_type=jnp.float32)
    key_part = jnp.dot(normal_rows, key_weight, preferred_element_type=jnp.float32)
    value_part = jnp.dot(normal_rows, value_weight, preferred_element_type=jnp.float32)
    query_full, key_full, value_full = (
        lax.psum_scatter(query_part, "mp", scatter_dimension=1, tiled=True),
        lax.psum_scatter(key_part, "mp", scatter_dimension=1, tiled=True),
        lax.psum_scatter(value_part, "mp", scatter_dimension=1, tiled=True),
    )
    offset_value = span_offset[0]
    local_iota = jnp.arange(row_count, dtype=jnp.int32)
    positions = jnp.where(
        decoding,
        offset_value + row_count * ctx_count + local_iota % STEPS,
        offset_value + ctx_index * row_count + local_iota,
    )
    queries = rotate(query_full, positions).astype(jnp.bfloat16)
    new_keys = rotate(key_full, positions).astype(jnp.bfloat16)
    new_values = value_full.astype(jnp.bfloat16)
    width = queries.shape[1]
    head_count = width // HD
    span_keys, span_values = passed_along((new_keys, new_values), "group", 1)
    block_keys = jnp.where(decoding, span_keys, new_keys)
    block_values = jnp.where(decoding, span_values, new_values)
    cache_count = cache_keys.shape[0]
    all_keys = jnp.concatenate([cache_keys, block_keys], 0)
    all_values = jnp.concatenate([cache_values, block_values], 0)
    live_length = shard_lengths[0]
    span_base = ctx_index * row_count
    gathered = lax.all_gather(queries, "ctx", axis=0, tiled=True)
    total = gathered.shape[0]
    block_rows = math.gcd(total, 512)
    block_count = total // block_rows
    block_starts = jnp.arange(block_count, dtype=jnp.int32) * block_rows

    def one_block(pair):
        return block_partial(
            pair[0], pair[1], all_keys, all_values, live_length, span_base, cache_count, decoding
        )

    maxima, totals, sums = lax.map(
        one_block, (gathered.reshape(block_count, block_rows, width), block_starts)
    )
    maxima = maxima.reshape(total, head_count)
    totals = totals.reshape(total, head_count)
    sums = sums.reshape(total, width)
    got_max, got_sum, got_acc = (
        lax.all_to_all(maxima[None], "ctx", split_axis=1, concat_axis=0, tiled=True),
        lax.all_to_all(totals[None], "ctx", split_axis=1, concat_axis=0, tiled=True),
        lax.all_to_all(sums[None], "ctx", split_axis=1, concat_axis=0, tiled=True),
    )
    whole_max = jnp.max(got_max, 0)
    rescale = jnp.exp(got_max - whole_max[None])
    whole_sum = jnp.sum(rescale * got_sum, 0)
    whole_acc = jnp.sum(got_acc * jnp.repeat(rescale, HD, axis=2), 0)
    cands = row_count // STEPS
    own_q = queries.reshape(cands, STEPS, head_count, HD)
    own_k = new_keys.reshape(cands, STEPS, head_count, HD)
    own_v = new_values.reshape(cands, STEPS, head_count, HD)
    own_scores = jnp.einsum("ashd,athd->ahst", own_q, own_k, preferred_element_type=jnp.float32) * (
        1.0 / math.sqrt(HD)
    )
    step_iota = jnp.arange(STEPS, dtype=jnp.int32)
    own_visible = (step_iota[None, :] <= step_iota[:, None]) & decoding
    own_max = jnp.max(jnp.where(own_visible, own_scores, -1e30), -1)
    final_max = jnp.maximum(whole_max, own_max.transpose(0, 2, 1).reshape(row_count, head_count))
    keep_old = jnp.exp(whole_max - final_max)
    final_cand = final_max.reshape(cands, STEPS, head_count).transpose(0, 2, 1)
    own_weights = jnp.where(own_visible, jnp.exp(own_scores - final_cand[..., None]), 0.0)
    own_sum = jnp.sum(own_weights, -1).transpose(0, 2, 1).reshape(row_count, head_count)
    own_acc = jnp.einsum(
        "ahst,athd->ashd",
        own_weights.astype(jnp.bfloat16),
        own_v,
        preferred_element_type=jnp.float32,
    ).reshape(row_count, width)
    numer = whole_acc * jnp.repeat(keep_old, HD, axis=1) + own_acc
    denom = whole_sum * keep_old + own_sum
    output = numer / jnp.repeat(denom, HD, axis=1)
    return output.astype(jnp.bfloat16)[None]


MESH_ID = pl.DeviceIdType.MESH
WINDOW = 256
ROW_BLOCK = 128
HIDDEN = -1e30


def flipped(index, mask):
    result = index
    bit = 1
    while bit <= mask:
        if mask & bit:
            result = result + bit * (1 - 2 * (index // bit % 2))
        bit *= 2
    return result


def masked_weights(scores, top):
    return jnp.exp2((scores - top) * (math.log2(math.e) / math.sqrt(HD)))


def across(left, right):
    return lax.dot_general(
        left, right, (((1,), (1,)), ((), ())), preferred_element_type=jnp.float32
    )


def layer_kernel(
    offset, length_here, packed, token_line, embed, gain, frequency, wq, wk, wv, got,
    kv, note, notes, wbuf, ss_out, ss_in, part_out, part_in, table, cosine, sine, query, own_key,
    own_value, span_key, span_value, first_max, first_sum, first_acc, scores, bias, out_parts,
    wsem, own_sem, note_send, note_recv, send_sem, recv_sem, relay_send, relay_recv, mp_send,
    mp_recv, out_send, out_recv, out_own,
):
    count, width, keep = packed.shape
    row_count = note.shape[1]
    rows = row_count * count
    vocab = embed.shape[0]
    group, ctx, mp = lax.axis_index("group"), lax.axis_index("ctx"), lax.axis_index("mp")
    decoding = group == 1
    half = wq.shape[1] // 2
    first = pl.multiple_of(ctx * width // 128 * 128, 128)
    near_first = sorted(range(1, count), key=lambda mask: mask)
    note_line = lax.broadcasted_iota(jnp.int32, note.shape, 0)
    note[...] = jnp.where(note_line == 0, token_line[...], length_here[0])
    barrier = pltpu.get_barrier_semaphore()
    for mask in near_first:
        for side in (group, 1 - group):
            pl.semaphore_signal(
                barrier,
                inc=1,
                device_id={"ctx": flipped(ctx, mask), "group": side},
                device_id_type=MESH_ID,
            )
    pl.semaphore_signal(barrier, inc=1, device_id={"group": 1 - group}, device_id_type=MESH_ID)
    pl.semaphore_signal(barrier, inc=1, device_id={"mp": 1 - mp}, device_id_type=MESH_ID)
    loads = []
    for slot in range(6):
        side = 1 - mp if slot < 3 else mp
        weight = (wq, wk, wv)[slot % 3]
        column = pl.multiple_of(side * half + first, 128)
        loads.append(
            pltpu.make_async_copy(
                weight.at[:, pl.ds(column, WINDOW)], wbuf.at[slot], wsem.at[slot]
            )
        )
        loads[-1].start()
    mine = pltpu.make_async_copy(packed.at[ctx], kv.at[group, ctx], own_sem.at[0])
    mine.start()
    my_note = pltpu.make_async_copy(note, notes.at[group, ctx], own_sem.at[1])
    my_note.start()
    embedded = embed[...].astype(jnp.float32)
    ss_out[...] = jnp.broadcast_to(jnp.sum(embedded * embedded, 1, keepdims=True), ss_out.shape)
    pl.semaphore_wait(barrier, 2 * count)
    squares = pltpu.make_async_remote_copy(
        src_ref=ss_out,
        dst_ref=ss_in,
        send_sem=mp_send.at[0],
        recv_sem=mp_recv.at[0],
        device_id={"mp": 1 - mp},
        device_id_type=MESH_ID,
    )
    squares.start()
    note_copies = []
    for mask in range(count):
        for same in (True, False):
            if mask == 0 and same:
                continue
            slot = 2 * mask + (0 if same else 1)
            note_copies.append(
                pltpu.make_async_remote_copy(
                    src_ref=note,
                    dst_ref=notes.at[group, ctx],
                    send_sem=note_send.at[slot],
                    recv_sem=note_recv.at[slot],
                    device_id={
                        "ctx": flipped(ctx, mask),
                        "group": group if same else 1 - group,
                    },
                    device_id_type=MESH_ID,
                )
            )
            note_copies[-1].start()
    sends = {}
    for mask in near_first:
        target = flipped(ctx, mask)
        sends[mask] = pltpu.make_async_remote_copy(
            src_ref=packed.at[target],
            dst_ref=kv.at[group, ctx],
            send_sem=send_sem.at[mask],
            recv_sem=recv_sem.at[mask],
            device_id={"ctx": target},
            device_id_type=MESH_ID,
        )
        sends[mask].start()
    relays = [
        pltpu.make_async_remote_copy(
            src_ref=packed.at[ctx],
            dst_ref=kv.at[group, ctx],
            send_sem=relay_send.at[0],
            recv_sem=relay_recv.at[0],
            device_id={"group": 1 - group},
            device_id_type=MESH_ID,
        )
    ]
    relays[0].start()

    def relay(mask):
        source = flipped(ctx, mask)
        sends[mask].wait_recv()
        relays.append(
            pltpu.make_async_remote_copy(
                src_ref=kv.at[group, source],
                dst_ref=kv.at[group, source],
                send_sem=relay_send.at[mask],
                recv_sem=relay_recv.at[mask],
                device_id={"group": 1 - group},
                device_id_type=MESH_ID,
            )
        )
        relays[-1].start()

    squares.wait()
    square_sum = (ss_out[...] + ss_in[...])[:, :1]
    normal = (
        embedded * lax.rsqrt(square_sum / D + 1e-05) * gain[...].astype(jnp.float32)[None]
    ).astype(jnp.bfloat16)
    for slot in range(3):
        loads[slot].wait()
        part_out[slot] = jnp.dot(normal, wbuf[slot], preferred_element_type=jnp.float32)
    parts = pltpu.make_async_remote_copy(
        src_ref=part_out,
        dst_ref=part_in,
        send_sem=mp_send.at[1],
        recv_sem=mp_recv.at[1],
        device_id={"mp": 1 - mp},
        device_id_type=MESH_ID,
    )
    parts.start()
    for slot in range(3):
        loads[slot + 3].wait()
        table[slot] = jnp.dot(normal, wbuf[slot + 3], preferred_element_type=jnp.float32)

    def turn(at, size, column, homolog, lane):
        angle = jnp.where(lane % HD >= HD // 2, homolog, column).astype(jnp.float32)
        angle = angle * frequency[...]
        cosine[pl.ds(at, size)] = jnp.cos(angle)
        sine[pl.ds(at, size)] = jnp.sin(angle)

    small = lax.broadcasted_iota(jnp.int32, (8, width), 0)
    small_lane = lax.broadcasted_iota(jnp.int32, (8, width), 1)
    homolog = offset[0] // PROT + small
    turn(PROT, 8, homolog, homolog, small_lane)
    position = offset[0] + rows + small % STEPS
    turn(PROT + 8, 8, position % PROT, position // PROT, small_lane)

    @pl.loop(0, PROT // 64)
    def _(piece):
        at = pl.multiple_of(piece * 64, 64)
        column = (offset[0] + at + lax.broadcasted_iota(jnp.int32, (64, width), 0)) % PROT
        turn(at, 64, column, column, lax.broadcasted_iota(jnp.int32, (64, width), 1))

    my_note.wait()
    for copy in note_copies:
        copy.wait()
    for source in range(count):
        length = notes[0, source, 1:2, :]
        for at in range(0, keep, 128):
            slot = lax.broadcasted_iota(jnp.int32, (1, 128), 1) + at
            bias[source : source + 1, at : at + 128] = jnp.where(slot < length, 0.0, HIDDEN)
    parts.wait()
    shift = lax.rem(WINDOW - (ctx * width - first), WINDOW)
    lane = lax.broadcasted_iota(jnp.int32, (vocab, WINDOW), 1)
    even = lane % (HD // 2) < HD // 4
    tables = []
    for slot in range(3):
        whole = pltpu.roll(table[slot] + part_in[slot], shift, 1)
        tables.append(whole)
        if slot < 2:
            tables.append(
                jnp.where(
                    even,
                    -pltpu.roll(whole, WINDOW - HD // 4, 1),
                    pltpu.roll(whole, HD // 4, 1),
                )
            )
    stacks = []
    for whole in tables:
        high = whole.astype(jnp.bfloat16)
        rest = (whole - high.astype(jnp.float32)).astype(jnp.bfloat16)
        stacks.append(jnp.concatenate([high, rest], 0))
    value_table = tables[4].astype(jnp.bfloat16)

    def picked(hot, table_in):
        return jnp.dot(hot, table_in, preferred_element_type=jnp.float32)[:, :width]

    def hot_rows(lines):
        letter = lax.broadcasted_iota(jnp.int32, (vocab, row_count), 0)
        hots = [jnp.transpose((letter == line).astype(jnp.float32)) for line in lines]
        return jnp.concatenate(hots, 0).astype(jnp.bfloat16)

    turn_row = lax.broadcasted_iota(jnp.int32, (PROT, width), 0)
    turn_second = lax.broadcasted_iota(jnp.int32, (PROT, width), 1) % HD >= HD // 2
    wrapped = offset[0] % PROT + turn_row >= PROT
    lines_per = PROT // row_count
    for block in range(rows // PROT):
        here = slice(block * PROT, (block + 1) * PROT)
        lines = range(block * lines_per, (block + 1) * lines_per)
        span_turn, own_turn = [], []
        for angles in (cosine, sine):
            low = PROT + block
            homolog_part = jnp.where(wrapped, angles[low + 1 : low + 2], angles[low : low + 1])
            span_turn.append(jnp.where(turn_second, homolog_part, angles[:PROT]))
            steps = jnp.concatenate([angles[PROT + 8 : PROT + 16]] * (PROT // 8), 0)
            own_turn.append(jnp.where(decoding, steps, span_turn[-1]))
        hot = hot_rows([notes[0, line, 0:1, :] for line in lines])
        twice = jnp.concatenate([hot, hot], 1)
        span_key[here] = (
            picked(twice, stacks[2]) * span_turn[0] + picked(twice, stacks[3]) * span_turn[1]
        ).astype(jnp.bfloat16)
        span_value[here] = picked(hot, value_table).astype(jnp.bfloat16)
        hot = hot_rows([notes[group, line, 0:1, :] for line in lines])
        twice = jnp.concatenate([hot, hot], 1)
        query[here] = (
            picked(twice, stacks[0]) * own_turn[0] + picked(twice, stacks[1]) * own_turn[1]
        ).astype(jnp.bfloat16)
        own_key[here] = (
            picked(twice, stacks[2]) * own_turn[0] + picked(twice, stacks[3]) * own_turn[1]
        ).astype(jnp.bfloat16)
        own_value[here] = picked(hot, value_table).astype(jnp.bfloat16)

    heads = width // HD
    head_lane = lax.broadcasted_iota(jnp.int32, (ROW_BLOCK, width), 1)
    inside = [(head_lane >= head * HD) & (head_lane < (head + 1) * HD) for head in range(heads)]

    def one_head(block_query, head):
        return jnp.where(inside[head], block_query, jnp.zeros_like(block_query))

    row = lax.broadcasted_iota(jnp.int32, (ROW_BLOCK, rows), 0)
    col = lax.broadcasted_iota(jnp.int32, (ROW_BLOCK, rows), 1)
    own_row = lax.broadcasted_iota(jnp.int32, (ROW_BLOCK, ROW_BLOCK), 0)
    own_col = lax.broadcasted_iota(jnp.int32, (ROW_BLOCK, ROW_BLOCK), 1)
    own_limit = jnp.where(decoding, own_row, -1)
    own_seen = (own_row // STEPS == own_col // STEPS) & (own_col <= own_limit)
    blocks = rows // ROW_BLOCK
    pending = list(near_first)
    for block in range(blocks):
        here = slice(block * ROW_BLOCK, (block + 1) * ROW_BLOCK)
        limit = jnp.where(decoding, rows, row + block * ROW_BLOCK)
        tops, sums, accs = None, None, None
        for head in range(heads):
            head_query = one_head(query[here], head)
            span_scores = jnp.where(col <= limit, across(head_query, span_key[...]), HIDDEN)
            own_scores = jnp.where(own_seen, across(head_query, own_key[here]), HIDDEN)
            top = jnp.maximum(
                jnp.max(span_scores, 1, keepdims=True), jnp.max(own_scores, 1, keepdims=True)
            )
            span_weights = masked_weights(span_scores, top)
            own_weights = masked_weights(own_scores, top)
            total = jnp.sum(span_weights, 1, keepdims=True) + jnp.sum(
                own_weights, 1, keepdims=True
            )
            acc = jnp.dot(
                span_weights.astype(jnp.bfloat16), span_value[...],
                preferred_element_type=jnp.float32,
            ) + jnp.dot(
                own_weights.astype(jnp.bfloat16), own_value[here],
                preferred_element_type=jnp.float32,
            )
            if head == 0:
                tops, sums, accs = top, total, acc
            else:
                tops = jnp.where(inside[head], top, tops)
                sums = jnp.where(inside[head], total, sums)
                accs = jnp.where(inside[head], acc, accs)
        first_max[here], first_sum[here], first_acc[here] = tops, sums, accs
        for _ in range(-(-(count - 1) // blocks)):
            if pending:
                relay(pending.pop(0))
    mine.wait()
    for copy in relays:
        copy.wait()
    for mask in near_first:
        sends[mask].wait_send()

    per_block = ROW_BLOCK // row_count

    def out_copy(owner):
        return pltpu.make_async_remote_copy(
            src_ref=out_parts.at[owner],
            dst_ref=got.at[ctx],
            send_sem=out_send.at[owner],
            recv_sem=out_recv.at[ctx],
            device_id={"ctx": owner},
            device_id_type=MESH_ID,
        )

    @pl.loop(0, blocks)
    def _(turn):
        block = lax.rem(ctx // per_block + 1 + turn, blocks)
        at = pl.multiple_of(block * ROW_BLOCK, ROW_BLOCK)
        here = pl.ds(at, ROW_BLOCK)
        block_query = query[here, :]
        old_top, old_sum, old_acc = first_max[here, :], first_sum[here, :], first_acc[here, :]
        result = None
        for head in range(heads):
            head_query = one_head(block_query, head)
            for source in range(count):
                part = jnp.dot(head_query, kv[0, source], preferred_element_type=jnp.float32)
                scores[:, source * keep : (source + 1) * keep] = part + bias[source : source + 1]
            before = old_top[:, head * HD : head * HD + 1]
            top = jnp.maximum(jnp.max(scores[...], 1, keepdims=True), before)
            ratio = masked_weights(before, top)
            total = old_sum[:, head * HD : head * HD + 1] * ratio
            acc = old_acc * ratio
            for source in range(count):
                weights = masked_weights(scores[:, source * keep : (source + 1) * keep], top)
                total += jnp.sum(weights, 1, keepdims=True)
                acc += across(weights.astype(jnp.bfloat16), kv[1, source])
            head_out = acc / total
            result = head_out if head == 0 else jnp.where(inside[head], head_out, result)
        padded = jnp.concatenate(
            [result, jnp.zeros((ROW_BLOCK, -width % 128), jnp.float32)], 1
        )
        turned = jnp.transpose(padded)[:width].astype(jnp.bfloat16)
        for piece in range(per_block):
            owner = block * per_block + piece
            out_parts[owner] = turned[:, piece * row_count : (piece + 1) * row_count]

            @pl.when(owner != ctx)
            def _():
                out_copy(owner).start()

            @pl.when(owner == ctx)
            def _():
                pltpu.make_async_copy(out_parts.at[ctx], got.at[ctx], out_own).start()

    pltpu.make_async_copy(out_parts.at[ctx], got.at[ctx], out_own).wait()
    for mask in near_first:
        peer = flipped(ctx, mask)
        arrival = pltpu.make_async_remote_copy(
            src_ref=out_parts.at[peer],
            dst_ref=got.at[peer],
            send_sem=out_send.at[peer],
            recv_sem=out_recv.at[peer],
            device_id={"ctx": peer},
            device_id_type=MESH_ID,
        )
        arrival.wait()


def layer(offset, length_here, packed, token_line, embed, gain, frequency, wq, wk, wv):
    count, width, keep = packed.shape
    row_count = token_line.shape[1]
    rows = row_count * count
    vocab, features = embed.shape
    vmem = pl.BlockSpec(memory_space=pltpu.VMEM)
    anywhere = pl.BlockSpec(memory_space=pl.ANY)
    wide, narrow = jnp.float32, jnp.bfloat16
    dma = pltpu.SemaphoreType.DMA
    return pl.pallas_call(
        layer_kernel,
        out_shape=jax.ShapeDtypeStruct((count, width, row_count), narrow),
        in_specs=[pl.BlockSpec(memory_space=pltpu.SMEM)] * 2 + [anywhere] + [vmem] * 4
        + [anywhere] * 3,
        out_specs=vmem,
        scratch_shapes=[
            pltpu.VMEM((2, count, width, keep), narrow),
            pltpu.VMEM((8, row_count), jnp.int32),
            pltpu.VMEM((2, count, 8, row_count), jnp.int32),
            pltpu.VMEM((6, features, WINDOW), narrow),
            pltpu.VMEM((vocab, 128), wide),
            pltpu.VMEM((vocab, 128), wide),
            pltpu.VMEM((3, vocab, WINDOW), wide),
            pltpu.VMEM((3, vocab, WINDOW), wide),
            pltpu.VMEM((3, vocab, WINDOW), wide),
            pltpu.VMEM((PROT + 16, width), wide),
            pltpu.VMEM((PROT + 16, width), wide),
            pltpu.VMEM((rows, width), narrow),
            pltpu.VMEM((rows, width), narrow),
            pltpu.VMEM((rows, width), narrow),
            pltpu.VMEM((rows, width), narrow),
            pltpu.VMEM((rows, width), narrow),
            pltpu.VMEM((rows, width), wide),
            pltpu.VMEM((rows, width), wide),
            pltpu.VMEM((rows, width), wide),
            pltpu.VMEM((ROW_BLOCK, count * keep), wide),
            pltpu.VMEM((count, keep), wide),
            pltpu.VMEM((count, width, row_count), narrow),
            dma((6,)),
            dma((2,)),
            dma((2 * count,)),
            dma((2 * count,)),
            dma((count,)),
            dma((count,)),
            dma((count,)),
            dma((count,)),
            dma((2,)),
            dma((2,)),
            dma((count,)),
            dma((count,)),
            dma,
        ],
        compiler_params=pltpu.CompilerParams(
            collective_id=0, has_side_effects=True, vmem_limit_bytes=56 << 20
        ),
        name="layer",
    )(offset, length_here, packed, token_line, embed, gain, frequency, wq, wk, wv)


def by_heads(
    token_ids,
    span_offset,
    shard_lengths,
    embed_table,
    norm_gain,
    query_weight,
    key_weight,
    value_weight,
    cache_keys,
    cache_values,
):
    row_count = token_ids.shape[1]
    count = lax.axis_size("ctx")
    cache_count, local_width = cache_keys.shape
    width = local_width // count
    decoding = lax.axis_index("group") == 1
    packed = jnp.where(decoding, cache_values, cache_keys).T.reshape(count, width, cache_count)
    quarter = HD // 4
    frequency = np.power(10000.0, -np.arange(quarter) / quarter).astype(np.float32)
    frequency = jnp.asarray(np.tile(frequency, width // quarter)[None])
    out = layer(
        span_offset, shard_lengths, packed, token_ids, embed_table, norm_gain, frequency,
        query_weight, key_weight, value_weight,
    )
    return out.reshape(local_width, row_count).T[None]


def solution(mesh):
    placed = (
        P("group", "ctx"),
        P(),
        P("ctx"),
        P(None, "mp"),
        P("mp"),
        P("mp", None),
        P("mp", None),
        P("mp", None),
        P("ctx", "mp"),
        P("ctx", "mp"),
    )
    heads = D // HD // mesh.shape["mp"]
    count = mesh.shape["ctx"]
    fits = heads == 2 * count and count == 8
    body = by_heads if fits else local
    return jax.shard_map(
        body, mesh=mesh, in_specs=placed, out_specs=P("group", "ctx", "mp"), check_vma=False
    )
```

```python
import math

import jax
import jax.numpy as jnp
import numpy as np
from jax import lax
from jax.experimental import pallas as pl
from jax.experimental.pallas import tpu as pltpu
from jax.sharding import PartitionSpec as P

D = 2560
HD = 80
PROT = 256
STEPS = 4


def passed_along(value, axis, steps):
    count = lax.axis_size(axis)
    first, last = (max(0, -steps), min(count, count - steps))
    return lax.ppermute(value, axis, [(source, source + steps) for source in range(first, last)])


def rotate(values_in, positions):
    row_count = values_in.shape[0]
    head_count = values_in.shape[1] // HD
    quarter = HD // 4
    column = (positions % PROT).astype(jnp.float32)
    homolog = (positions // PROT).astype(jnp.float32)
    frequency = 10000.0 ** (-jnp.arange(quarter, dtype=jnp.float32) / quarter)
    angles = jnp.stack([column[:, None] * frequency, homolog[:, None] * frequency], 1)
    cosine = jnp.cos(angles)[:, None, :, None, :]
    sine_table = jnp.sin(angles)[:, None, :, None, :]
    pieces = values_in.reshape(row_count, head_count, 2, 2, quarter)
    partner = jnp.stack([-pieces[:, :, :, 1], pieces[:, :, :, 0]], 3)
    return (pieces * cosine + partner * sine_table).reshape(row_count, head_count * HD)


def block_partial(
    query_block, start, all_keys, all_values, live_length, span_base, cache_count, decoding
):
    block_rows = query_block.shape[0]
    head_count = query_block.shape[1] // HD
    key_slots = all_keys.shape[0]
    query_heads = query_block.reshape(block_rows, head_count, HD)
    key_heads = all_keys.reshape(key_slots, head_count, HD)
    value_heads = all_values.reshape(key_slots, head_count, HD)
    scores = jnp.einsum(
        "qhd,khd->hqk", query_heads, key_heads, preferred_element_type=jnp.float32
    ) * (1.0 / math.sqrt(HD))
    slot = jnp.arange(key_slots, dtype=jnp.int32)
    query_index = start + jnp.arange(block_rows, dtype=jnp.int32)
    cache_live = (slot < cache_count) & (slot < live_length)
    span_index = span_base + slot - cache_count
    span_seen = (slot >= cache_count)[None, :] & (
        decoding | (span_index[None, :] <= query_index[:, None])
    )
    visible = (cache_live[None, :] | span_seen)[None]
    block_max = jnp.max(jnp.where(visible, scores, -1e30), -1)
    weights = jnp.where(visible, jnp.exp(scores - block_max[..., None]), 0.0)
    block_sum = jnp.sum(weights, -1)
    block_acc = jnp.einsum(
        "hqk,khd->qhd",
        weights.astype(jnp.bfloat16),
        value_heads,
        preferred_element_type=jnp.float32,
    )
    return (block_max.T, block_sum.T, block_acc.reshape(block_rows, head_count * HD))


def local(
    token_ids,
    span_offset,
    shard_lengths,
    embed_table,
    norm_gain,
    query_weight,
    key_weight,
    value_weight,
    cache_keys,
    cache_values,
):
    token_row = token_ids[0]
    row_count = token_row.shape[0]
    ctx_count = lax.axis_size("ctx")
    ctx_index = lax.axis_index("ctx")
    decoding = lax.axis_index("group") == 1
    one_hot = (
        token_row[:, None] == jnp.arange(embed_table.shape[0], dtype=jnp.int32)[None, :]
    ).astype(jnp.bfloat16)
    embedded = jnp.dot(one_hot, embed_table, preferred_element_type=jnp.float32)
    square_sum = lax.psum(jnp.sum(embedded * embedded, 1), "mp")
    normal_rows = (
        embedded * lax.rsqrt(square_sum / D + 1e-05)[:, None] * norm_gain.astype(jnp.float32)
    ).astype(jnp.bfloat16)
    query_part = jnp.dot(normal_rows, query_weight, preferred_element_type=jnp.float32)
    key_part = jnp.dot(normal_rows, key_weight, preferred_element_type=jnp.float32)
    value_part = jnp.dot(normal_rows, value_weight, preferred_element_type=jnp.float32)
    query_full, key_full, value_full = (
        lax.psum_scatter(query_part, "mp", scatter_dimension=1, tiled=True),
        lax.psum_scatter(key_part, "mp", scatter_dimension=1, tiled=True),
        lax.psum_scatter(value_part, "mp", scatter_dimension=1, tiled=True),
    )
    offset_value = span_offset[0]
    local_iota = jnp.arange(row_count, dtype=jnp.int32)
    positions = jnp.where(
        decoding,
        offset_value + row_count * ctx_count + local_iota % STEPS,
        offset_value + ctx_index * row_count + local_iota,
    )
    queries = rotate(query_full, positions).astype(jnp.bfloat16)
    new_keys = rotate(key_full, positions).astype(jnp.bfloat16)
    new_values = value_full.astype(jnp.bfloat16)
    width = queries.shape[1]
    head_count = width // HD
    span_keys, span_values = passed_along((new_keys, new_values), "group", 1)
    block_keys = jnp.where(decoding, span_keys, new_keys)
    block_values = jnp.where(decoding, span_values, new_values)
    cache_count = cache_keys.shape[0]
    all_keys = jnp.concatenate([cache_keys, block_keys], 0)
    all_values = jnp.concatenate([cache_values, block_values], 0)
    live_length = shard_lengths[0]
    span_base = ctx_index * row_count
    gathered = lax.all_gather(queries, "ctx", axis=0, tiled=True)
    total = gathered.shape[0]
    block_rows = math.gcd(total, 512)
    block_count = total // block_rows
    block_starts = jnp.arange(block_count, dtype=jnp.int32) * block_rows

    def one_block(pair):
        return block_partial(
            pair[0], pair[1], all_keys, all_values, live_length, span_base, cache_count, decoding
        )

    maxima, totals, sums = lax.map(
        one_block, (gathered.reshape(block_count, block_rows, width), block_starts)
    )
    maxima = maxima.reshape(total, head_count)
    totals = totals.reshape(total, head_count)
    sums = sums.reshape(total, width)
    got_max, got_sum, got_acc = (
        lax.all_to_all(maxima[None], "ctx", split_axis=1, concat_axis=0, tiled=True),
        lax.all_to_all(totals[None], "ctx", split_axis=1, concat_axis=0, tiled=True),
        lax.all_to_all(sums[None], "ctx", split_axis=1, concat_axis=0, tiled=True),
    )
    whole_max = jnp.max(got_max, 0)
    rescale = jnp.exp(got_max - whole_max[None])
    whole_sum = jnp.sum(rescale * got_sum, 0)
    whole_acc = jnp.sum(got_acc * jnp.repeat(rescale, HD, axis=2), 0)
    cands = row_count // STEPS
    own_q = queries.reshape(cands, STEPS, head_count, HD)
    own_k = new_keys.reshape(cands, STEPS, head_count, HD)
    own_v = new_values.reshape(cands, STEPS, head_count, HD)
    own_scores = jnp.einsum("ashd,athd->ahst", own_q, own_k, preferred_element_type=jnp.float32) * (
        1.0 / math.sqrt(HD)
    )
    step_iota = jnp.arange(STEPS, dtype=jnp.int32)
    own_visible = (step_iota[None, :] <= step_iota[:, None]) & decoding
    own_max = jnp.max(jnp.where(own_visible, own_scores, -1e30), -1)
    final_max = jnp.maximum(whole_max, own_max.transpose(0, 2, 1).reshape(row_count, head_count))
    keep_old = jnp.exp(whole_max - final_max)
    final_cand = final_max.reshape(cands, STEPS, head_count).transpose(0, 2, 1)
    own_weights = jnp.where(own_visible, jnp.exp(own_scores - final_cand[..., None]), 0.0)
    own_sum = jnp.sum(own_weights, -1).transpose(0, 2, 1).reshape(row_count, head_count)
    own_acc = jnp.einsum(
        "ahst,athd->ashd",
        own_weights.astype(jnp.bfloat16),
        own_v,
        preferred_element_type=jnp.float32,
    ).reshape(row_count, width)
    numer = whole_acc * jnp.repeat(keep_old, HD, axis=1) + own_acc
    denom = whole_sum * keep_old + own_sum
    output = numer / jnp.repeat(denom, HD, axis=1)
    return output.astype(jnp.bfloat16)[None]


MESH_ID = pl.DeviceIdType.MESH
WINDOW = 256
ROW_BLOCK = 128
HIDDEN = -1e30


def flipped(index, mask):
    result = index
    bit = 1
    while bit <= mask:
        if mask & bit:
            result = result + bit * (1 - 2 * (index // bit % 2))
        bit *= 2
    return result


def masked_weights(scores, top):
    return jnp.exp2((scores - top) * (math.log2(math.e) / math.sqrt(HD)))


def across(left, right):
    return lax.dot_general(
        left, right, (((1,), (1,)), ((), ())), preferred_element_type=jnp.float32
    )


def layer_kernel(
    offset, length_here, packed, token_line, embed, gain, frequency, wq, wk, wv, got,
    kv, note, notes, wbuf, ss_out, ss_in, part_out, part_in, table, cosine, sine, query, own_key,
    own_value, span_key, span_value, first_max, first_sum, first_acc, scores, bias, out_parts,
    wsem, own_sem, note_send, note_recv, send_sem, recv_sem, relay_send, relay_recv, mp_send,
    mp_recv, out_send, out_recv, out_own,
):
    count, width, keep = packed.shape
    row_count = note.shape[1]
    rows = row_count * count
    vocab = embed.shape[0]
    group, ctx, mp = lax.axis_index("group"), lax.axis_index("ctx"), lax.axis_index("mp")
    decoding = group == 1
    half = wq.shape[1] // 2
    first = pl.multiple_of(ctx * width // 128 * 128, 128)
    near_first = sorted(range(1, count), key=lambda mask: mask)
    note_line = lax.broadcasted_iota(jnp.int32, note.shape, 0)
    note[...] = jnp.where(note_line == 0, token_line[...], length_here[0])
    barrier = pltpu.get_barrier_semaphore()
    for mask in near_first:
        for side in (group, 1 - group):
            pl.semaphore_signal(
                barrier,
                inc=1,
                device_id={"ctx": flipped(ctx, mask), "group": side},
                device_id_type=MESH_ID,
            )
    pl.semaphore_signal(barrier, inc=1, device_id={"group": 1 - group}, device_id_type=MESH_ID)
    pl.semaphore_signal(barrier, inc=1, device_id={"mp": 1 - mp}, device_id_type=MESH_ID)
    loads = []
    for slot in range(6):
        side = 1 - mp if slot < 3 else mp
        weight = (wq, wk, wv)[slot % 3]
        column = pl.multiple_of(side * half + first, 128)
        loads.append(
            pltpu.make_async_copy(
                weight.at[:, pl.ds(column, WINDOW)], wbuf.at[slot], wsem.at[slot]
            )
        )
        loads[-1].start()
    mine = pltpu.make_async_copy(packed.at[ctx], kv.at[group, ctx], own_sem.at[0])
    mine.start()
    my_note = pltpu.make_async_copy(note, notes.at[group, ctx], own_sem.at[1])
    my_note.start()
    embedded = embed[...].astype(jnp.float32)
    ss_out[...] = jnp.broadcast_to(jnp.sum(embedded * embedded, 1, keepdims=True), ss_out.shape)
    pl.semaphore_wait(barrier, 2 * count)
    squares = pltpu.make_async_remote_copy(
        src_ref=ss_out,
        dst_ref=ss_in,
        send_sem=mp_send.at[0],
        recv_sem=mp_recv.at[0],
        device_id={"mp": 1 - mp},
        device_id_type=MESH_ID,
    )
    squares.start()
    note_copies = []
    for mask in range(count):
        for same in (True, False):
            if mask == 0 and same:
                continue
            slot = 2 * mask + (0 if same else 1)
            note_copies.append(
                pltpu.make_async_remote_copy(
                    src_ref=note,
                    dst_ref=notes.at[group, ctx],
                    send_sem=note_send.at[slot],
                    recv_sem=note_recv.at[slot],
                    device_id={
                        "ctx": flipped(ctx, mask),
                        "group": group if same else 1 - group,
                    },
                    device_id_type=MESH_ID,
                )
            )
            note_copies[-1].start()
    sends = {}
    for mask in near_first:
        target = flipped(ctx, mask)
        sends[mask] = pltpu.make_async_remote_copy(
            src_ref=packed.at[target],
            dst_ref=kv.at[group, ctx],
            send_sem=send_sem.at[mask],
            recv_sem=recv_sem.at[mask],
            device_id={"ctx": target},
            device_id_type=MESH_ID,
        )
        sends[mask].start()
    relays = [
        pltpu.make_async_remote_copy(
            src_ref=packed.at[ctx],
            dst_ref=kv.at[group, ctx],
            send_sem=relay_send.at[0],
            recv_sem=relay_recv.at[0],
            device_id={"group": 1 - group},
            device_id_type=MESH_ID,
        )
    ]
    relays[0].start()

    def relay(mask):
        source = flipped(ctx, mask)
        sends[mask].wait_recv()
        relays.append(
            pltpu.make_async_remote_copy(
                src_ref=kv.at[group, source],
                dst_ref=kv.at[group, source],
                send_sem=relay_send.at[mask],
                recv_sem=relay_recv.at[mask],
                device_id={"group": 1 - group},
                device_id_type=MESH_ID,
            )
        )
        relays[-1].start()

    squares.wait()
    square_sum = (ss_out[...] + ss_in[...])[:, :1]
    normal = (
        embedded * lax.rsqrt(square_sum / D + 1e-05) * gain[...].astype(jnp.float32)[None]
    ).astype(jnp.bfloat16)
    mine_rows = pl.ds(pl.multiple_of(group * (vocab // 2), 8), vocab // 2)
    parts, part_relays = [], []
    for slot in range(3):
        loads[slot].wait()
        part_out[slot] = jnp.dot(normal, wbuf[slot], preferred_element_type=jnp.float32)
        parts.append(
            pltpu.make_async_remote_copy(
                src_ref=part_out.at[slot, mine_rows],
                dst_ref=part_in.at[slot, mine_rows],
                send_sem=mp_send.at[1 + slot],
                recv_sem=mp_recv.at[1 + slot],
                device_id={"mp": 1 - mp},
                device_id_type=MESH_ID,
            )
        )
        parts[-1].start()
        part_relays.append(
            pltpu.make_async_remote_copy(
                src_ref=part_in.at[slot, mine_rows],
                dst_ref=part_in.at[slot, mine_rows],
                send_sem=mp_send.at[4 + slot],
                recv_sem=mp_recv.at[4 + slot],
                device_id={"group": 1 - group},
                device_id_type=MESH_ID,
            )
        )
    for slot in range(3):
        loads[slot + 3].wait()
        table[slot] = jnp.dot(normal, wbuf[slot + 3], preferred_element_type=jnp.float32)

    def turn(at, size, column, homolog, lane):
        angle = jnp.where(lane % HD >= HD // 2, homolog, column).astype(jnp.float32)
        angle = angle * frequency[...]
        cosine[pl.ds(at, size)] = jnp.cos(angle)
        sine[pl.ds(at, size)] = jnp.sin(angle)

    small = lax.broadcasted_iota(jnp.int32, (8, width), 0)
    small_lane = lax.broadcasted_iota(jnp.int32, (8, width), 1)
    homolog = offset[0] // PROT + small
    turn(PROT, 8, homolog, homolog, small_lane)
    position = offset[0] + rows + small % STEPS
    turn(PROT + 8, 8, position % PROT, position // PROT, small_lane)

    @pl.loop(0, PROT // 64)
    def _(piece):
        at = pl.multiple_of(piece * 64, 64)
        column = (offset[0] + at + lax.broadcasted_iota(jnp.int32, (64, width), 0)) % PROT
        turn(at, 64, column, column, lax.broadcasted_iota(jnp.int32, (64, width), 1))

    my_note.wait()
    for copy in note_copies:
        copy.wait()
    for source in range(count):
        length = notes[0, source, 1:2, :]
        for at in range(0, keep, 128):
            slot = lax.broadcasted_iota(jnp.int32, (1, 128), 1) + at
            bias[source : source + 1, at : at + 128] = jnp.where(slot < length, 0.0, HIDDEN)
    for slot in range(3):
        parts[slot].wait()
        part_relays[slot].start()
    for copy in part_relays:
        copy.wait()
    shift = lax.rem(WINDOW - (ctx * width - first), WINDOW)
    lane = lax.broadcasted_iota(jnp.int32, (vocab, WINDOW), 1)
    even = lane % (HD // 2) < HD // 4
    tables = []
    for slot in range(3):
        whole = pltpu.roll(table[slot] + part_in[slot], shift, 1)
        tables.append(whole)
        if slot < 2:
            tables.append(
                jnp.where(
                    even,
                    -pltpu.roll(whole, WINDOW - HD // 4, 1),
                    pltpu.roll(whole, HD // 4, 1),
                )
            )
    stacks = []
    for whole in tables:
        high = whole.astype(jnp.bfloat16)
        rest = (whole - high.astype(jnp.float32)).astype(jnp.bfloat16)
        stacks.append(jnp.concatenate([high, rest], 0))
    value_table = tables[4].astype(jnp.bfloat16)

    def picked(hot, table_in):
        return jnp.dot(hot, table_in, preferred_element_type=jnp.float32)[:, :width]

    def hot_rows(lines):
        letter = lax.broadcasted_iota(jnp.int32, (vocab, row_count), 0)
        hots = [jnp.transpose((letter == line).astype(jnp.float32)) for line in lines]
        return jnp.concatenate(hots, 0).astype(jnp.bfloat16)

    turn_row = lax.broadcasted_iota(jnp.int32, (PROT, width), 0)
    turn_second = lax.broadcasted_iota(jnp.int32, (PROT, width), 1) % HD >= HD // 2
    wrapped = offset[0] % PROT + turn_row >= PROT
    lines_per = PROT // row_count
    for block in range(rows // PROT):
        here = slice(block * PROT, (block + 1) * PROT)
        lines = range(block * lines_per, (block + 1) * lines_per)
        span_turn, own_turn = [], []
        for angles in (cosine, sine):
            low = PROT + block
            homolog_part = jnp.where(wrapped, angles[low + 1 : low + 2], angles[low : low + 1])
            span_turn.append(jnp.where(turn_second, homolog_part, angles[:PROT]))
            steps = jnp.concatenate([angles[PROT + 8 : PROT + 16]] * (PROT // 8), 0)
            own_turn.append(jnp.where(decoding, steps, span_turn[-1]))
        hot = hot_rows([notes[0, line, 0:1, :] for line in lines])
        twice = jnp.concatenate([hot, hot], 1)
        span_key[here] = (
            picked(twice, stacks[2]) * span_turn[0] + picked(twice, stacks[3]) * span_turn[1]
        ).astype(jnp.bfloat16)
        span_value[here] = picked(hot, value_table).astype(jnp.bfloat16)
        hot = hot_rows([notes[group, line, 0:1, :] for line in lines])
        twice = jnp.concatenate([hot, hot], 1)
        query[here] = (
            picked(twice, stacks[0]) * own_turn[0] + picked(twice, stacks[1]) * own_turn[1]
        ).astype(jnp.bfloat16)
        own_key[here] = (
            picked(twice, stacks[2]) * own_turn[0] + picked(twice, stacks[3]) * own_turn[1]
        ).astype(jnp.bfloat16)
        own_value[here] = picked(hot, value_table).astype(jnp.bfloat16)

    heads = width // HD
    head_lane = lax.broadcasted_iota(jnp.int32, (ROW_BLOCK, width), 1)
    inside = [(head_lane >= head * HD) & (head_lane < (head + 1) * HD) for head in range(heads)]

    def one_head(block_query, head):
        return jnp.where(inside[head], block_query, jnp.zeros_like(block_query))

    row = lax.broadcasted_iota(jnp.int32, (ROW_BLOCK, rows), 0)
    col = lax.broadcasted_iota(jnp.int32, (ROW_BLOCK, rows), 1)
    own_row = lax.broadcasted_iota(jnp.int32, (ROW_BLOCK, ROW_BLOCK), 0)
    own_col = lax.broadcasted_iota(jnp.int32, (ROW_BLOCK, ROW_BLOCK), 1)
    own_limit = jnp.where(decoding, own_row, -1)
    own_seen = (own_row // STEPS == own_col // STEPS) & (own_col <= own_limit)
    blocks = rows // ROW_BLOCK
    pending = list(near_first)
    for block in range(blocks):
        here = slice(block * ROW_BLOCK, (block + 1) * ROW_BLOCK)
        limit = jnp.where(decoding, rows, row + block * ROW_BLOCK)
        tops, sums, accs = None, None, None
        for head in range(heads):
            head_query = one_head(query[here], head)
            span_scores = jnp.where(col <= limit, across(head_query, span_key[...]), HIDDEN)
            own_scores = jnp.where(own_seen, across(head_query, own_key[here]), HIDDEN)
            top = jnp.maximum(
                jnp.max(span_scores, 1, keepdims=True), jnp.max(own_scores, 1, keepdims=True)
            )
            span_weights = masked_weights(span_scores, top)
            own_weights = masked_weights(own_scores, top)
            total = jnp.sum(span_weights, 1, keepdims=True) + jnp.sum(
                own_weights, 1, keepdims=True
            )
            acc = jnp.dot(
                span_weights.astype(jnp.bfloat16), span_value[...],
                preferred_element_type=jnp.float32,
            ) + jnp.dot(
                own_weights.astype(jnp.bfloat16), own_value[here],
                preferred_element_type=jnp.float32,
            )
            if head == 0:
                tops, sums, accs = top, total, acc
            else:
                tops = jnp.where(inside[head], top, tops)
                sums = jnp.where(inside[head], total, sums)
                accs = jnp.where(inside[head], acc, accs)
        first_max[here], first_sum[here], first_acc[here] = tops, sums, accs
        for _ in range(-(-(count - 1) // blocks)):
            if pending:
                relay(pending.pop(0))
    mine.wait()
    for copy in relays:
        copy.wait()
    for mask in near_first:
        sends[mask].wait_send()

    per_block = ROW_BLOCK // row_count

    def out_copy(owner):
        return pltpu.make_async_remote_copy(
            src_ref=out_parts.at[owner],
            dst_ref=got.at[ctx],
            send_sem=out_send.at[owner],
            recv_sem=out_recv.at[ctx],
            device_id={"ctx": owner},
            device_id_type=MESH_ID,
        )

    @pl.loop(0, blocks)
    def _(turn):
        block = lax.rem(ctx // per_block + 1 + turn, blocks)
        at = pl.multiple_of(block * ROW_BLOCK, ROW_BLOCK)
        here = pl.ds(at, ROW_BLOCK)
        block_query = query[here, :]
        old_top, old_sum, old_acc = first_max[here, :], first_sum[here, :], first_acc[here, :]
        result = None
        for head in range(heads):
            head_query = one_head(block_query, head)
            for source in range(count):
                part = jnp.dot(head_query, kv[0, source], preferred_element_type=jnp.float32)
                scores[:, source * keep : (source + 1) * keep] = part + bias[source : source + 1]
            before = old_top[:, head * HD : head * HD + 1]
            top = jnp.maximum(jnp.max(scores[...], 1, keepdims=True), before)
            ratio = masked_weights(before, top)
            total = old_sum[:, head * HD : head * HD + 1] * ratio
            acc = old_acc * ratio
            for source in range(count):
                weights = masked_weights(scores[:, source * keep : (source + 1) * keep], top)
                total += jnp.sum(weights, 1, keepdims=True)
                acc += across(weights.astype(jnp.bfloat16), kv[1, source])
            head_out = acc / total
            result = head_out if head == 0 else jnp.where(inside[head], head_out, result)
        padded = jnp.concatenate(
            [result, jnp.zeros((ROW_BLOCK, -width % 128), jnp.float32)], 1
        )
        turned = jnp.transpose(padded)[:width].astype(jnp.bfloat16)
        for piece in range(per_block):
            owner = block * per_block + piece
            out_parts[owner] = turned[:, piece * row_count : (piece + 1) * row_count]

            @pl.when(owner != ctx)
            def _():
                out_copy(owner).start()

            @pl.when(owner == ctx)
            def _():
                pltpu.make_async_copy(out_parts.at[ctx], got.at[ctx], out_own).start()

    pltpu.make_async_copy(out_parts.at[ctx], got.at[ctx], out_own).wait()
    for mask in near_first:
        peer = flipped(ctx, mask)
        arrival = pltpu.make_async_remote_copy(
            src_ref=out_parts.at[peer],
            dst_ref=got.at[peer],
            send_sem=out_send.at[peer],
            recv_sem=out_recv.at[peer],
            device_id={"ctx": peer},
            device_id_type=MESH_ID,
        )
        arrival.wait()


def layer(offset, length_here, packed, token_line, embed, gain, frequency, wq, wk, wv):
    count, width, keep = packed.shape
    row_count = token_line.shape[1]
    rows = row_count * count
    vocab, features = embed.shape
    vmem = pl.BlockSpec(memory_space=pltpu.VMEM)
    anywhere = pl.BlockSpec(memory_space=pl.ANY)
    wide, narrow = jnp.float32, jnp.bfloat16
    dma = pltpu.SemaphoreType.DMA
    return pl.pallas_call(
        layer_kernel,
        out_shape=jax.ShapeDtypeStruct((count, width, row_count), narrow),
        in_specs=[pl.BlockSpec(memory_space=pltpu.SMEM)] * 2 + [anywhere] + [vmem] * 4
        + [anywhere] * 3,
        out_specs=vmem,
        scratch_shapes=[
            pltpu.VMEM((2, count, width, keep), narrow),
            pltpu.VMEM((8, row_count), jnp.int32),
            pltpu.VMEM((2, count, 8, row_count), jnp.int32),
            pltpu.VMEM((6, features, WINDOW), narrow),
            pltpu.VMEM((vocab, 128), wide),
            pltpu.VMEM((vocab, 128), wide),
            pltpu.VMEM((3, vocab, WINDOW), wide),
            pltpu.VMEM((3, vocab, WINDOW), wide),
            pltpu.VMEM((3, vocab, WINDOW), wide),
            pltpu.VMEM((PROT + 16, width), wide),
            pltpu.VMEM((PROT + 16, width), wide),
            pltpu.VMEM((rows, width), narrow),
            pltpu.VMEM((rows, width), narrow),
            pltpu.VMEM((rows, width), narrow),
            pltpu.VMEM((rows, width), narrow),
            pltpu.VMEM((rows, width), narrow),
            pltpu.VMEM((rows, width), wide),
            pltpu.VMEM((rows, width), wide),
            pltpu.VMEM((rows, width), wide),
            pltpu.VMEM((ROW_BLOCK, count * keep), wide),
            pltpu.VMEM((count, keep), wide),
            pltpu.VMEM((count, width, row_count), narrow),
            dma((6,)),
            dma((2,)),
            dma((2 * count,)),
            dma((2 * count,)),
            dma((count,)),
            dma((count,)),
            dma((count,)),
            dma((count,)),
            dma((7,)),
            dma((7,)),
            dma((count,)),
            dma((count,)),
            dma,
        ],
        compiler_params=pltpu.CompilerParams(
            collective_id=0, has_side_effects=True, vmem_limit_bytes=56 << 20
        ),
        name="layer",
    )(offset, length_here, packed, token_line, embed, gain, frequency, wq, wk, wv)


def by_heads(
    token_ids,
    span_offset,
    shard_lengths,
    embed_table,
    norm_gain,
    query_weight,
    key_weight,
    value_weight,
    cache_keys,
    cache_values,
):
    row_count = token_ids.shape[1]
    count = lax.axis_size("ctx")
    cache_count, local_width = cache_keys.shape
    width = local_width // count
    decoding = lax.axis_index("group") == 1
    packed = jnp.where(decoding, cache_values, cache_keys).T.reshape(count, width, cache_count)
    quarter = HD // 4
    frequency = np.power(10000.0, -np.arange(quarter) / quarter).astype(np.float32)
    frequency = jnp.asarray(np.tile(frequency, width // quarter)[None])
    out = layer(
        span_offset, shard_lengths, packed, token_ids, embed_table, norm_gain, frequency,
        query_weight, key_weight, value_weight,
    )
    return out.reshape(local_width, row_count).T[None]


def solution(mesh):
    placed = (
        P("group", "ctx"),
        P(),
        P("ctx"),
        P(None, "mp"),
        P("mp"),
        P("mp", None),
        P("mp", None),
        P("mp", None),
        P("ctx", "mp"),
        P("ctx", "mp"),
    )
    heads = D // HD // mesh.shape["mp"]
    count = mesh.shape["ctx"]
    fits = heads == 2 * count and count == 8
    body = by_heads if fits else local
    return jax.shard_map(
        body, mesh=mesh, in_specs=placed, out_specs=P("group", "ctx", "mp"), check_vma=False
    )
```
